32 devices in a mesh: dp: 8 (over y, x, core), tensor: 4 (over z).
Axes of the slice: x: 2, y: 2, z: 4, core: 2. Of those that a mesh axis runs over, the one named last changes fastest.
Arguments:
- tokens: bfloat16 [32, 576, 768], P('dp'), may hold values from -6 to 6
- segments: int32 [32, 576], P('dp'), may hold values from 0 to 4, as said below
- cotangent: bfloat16 [32, 576, 768], P('dp'), may hold values from -6 to 6
- inproj: bfloat16 [768, 3, 768], P(None, None, 'tensor'), may hold values from -0.21875 to 0.21875
- querybias: bfloat16 [768], P('tensor'), may hold values from -4 to 4
- valuebias: bfloat16 [768], P('tensor'), may hold values from -0.75 to 0.75
- outproj: bfloat16 [768, 768], P('tensor'), may hold values from -2.5 to 2.5
- outbias: bfloat16 [768], replicated, may hold values from -6 to 6
- gainone: bfloat16 [768], replicated, may hold values from 0.25 to 1.75
- shiftone: bfloat16 [768], replicated, may hold values from -4 to 4
- gaintwo: bfloat16 [768], replicated, may hold values from 0.25 to 1.75
- shifttwo: bfloat16 [768], replicated, may hold values from -4 to 4
- expand: bfloat16 [768, 3072], P(None, 'tensor'), may hold values from -0.21875 to 0.21875
- expandbias: bfloat16 [3072], P('tensor'), may hold values from -6 to 6
- contract: bfloat16 [3072, 768], P('tensor'), may hold values from -0.109375 to 0.109375
- contractbias: bfloat16 [768], replicated, may hold values from -6 to 6
Outputs:
- layer_out: bfloat16 [32, 576, 768], P('dp')
- token_grad: bfloat16 [32, 576, 768], P('dp')
- inproj_grad: float32 [768, 3, 768], P(None, None, 'tensor')
- querybias_grad: float32 [768], P('tensor')
- valuebias_grad: float32 [768], P('tensor')
- outproj_grad: float32 [768, 768], P('tensor')
- outbias_grad: float32 [768], replicated
- gainone_grad: float32 [768], replicated
- shiftone_grad: float32 [768], replicated
- gaintwo_grad: float32 [768], replicated
- shifttwo_grad: float32 [768], replicated
- expand_grad: float32 [768, 3072], P(None, 'tensor')
- expandbias_grad: float32 [3072], P('tensor')
- contract_grad: float32 [3072, 768], P('tensor')
- contractbias_grad: float32 [768], replicated
The draws below stay inside these ranges and needn't reach their ends.
Inputs may be any that keep to these rules, and one draw needn't show every extreme that they name: `segments`: in every sequence, tiles numbered 1, 2, ... in order cover runs of 128 or more slots from the first slot on, two to four tiles a sequence; the remaining slots, at most 48, are padding with id 0. Some sequence has four tiles and 48 padding slots.
All inputs are finite; a program needn't handle non-finite values.
Results may differ from the reference program's by a relative error of at most 0.02.
Values may be sent and summed in bfloat16 or wider, within the bound.
A program may use at most 128 MiB of HBM per device.

```python
import jax
import jax.numpy as jnp
from jax import lax

D = 768
H = 12
HD = 64
FF = 3072
LEN = 576
TILE_MIN = 128
PAD_MAX = 48
SEQS = 32
N_TENSOR = 4


def draw_segments(key, part):
    subkeys = jax.random.split(key, 6)
    chosen = jax.random.randint(subkeys[0], (), 0, SEQS)
    is_chosen = jnp.arange(SEQS) == chosen
    padding = jax.random.randint(subkeys[1], (SEQS,), 0, PAD_MAX + 1)
    padding = jnp.where(is_chosen, PAD_MAX, padding)
    used_rows = LEN - padding
    remain = used_rows
    boundary = jnp.zeros((SEQS,), jnp.int32)
    position = jnp.arange(LEN)[None, :]
    tile_ids = jnp.ones((SEQS, LEN), jnp.int32)
    for tile_turn in range(4):
        upper_end = jnp.minimum(LEN, remain - TILE_MIN)
        span_rows = jnp.maximum(upper_end - TILE_MIN + 1, 1)
        raw_bits = jax.random.randint(subkeys[2 + tile_turn], (SEQS,), 0, 1 << 20)
        extent = TILE_MIN + raw_bits % span_rows
        extent = jnp.where(is_chosen, TILE_MIN, extent)
        extent = jnp.where(remain >= 2 * TILE_MIN, extent, remain)
        boundary = boundary + extent
        remain = remain - extent
        tile_ids = tile_ids + (position >= boundary[:, None]).astype(jnp.int32)
    return jnp.where(position < used_rows[:, None], tile_ids, 0)


def levels(own_key, shape, cuts, smallest, largest):
    def one(dim, parts):
        draws = jax.random.uniform(jax.random.fold_in(jax.random.fold_in(own_key, 6), dim), (parts,), jnp.float32, smallest / len(cuts), largest / len(cuts))
        return jnp.repeat(jnp.exp(draws), shape[dim] // parts).reshape((-1,) + (1,) * (len(shape) - dim - 1))

    factor_of = one(*cuts[0])
    for cut in cuts[1:]:
        factor_of = factor_of * one(*cut)
    return factor_of


def normal_values(rng, dims, scale, reach, cuts=(), kind=jnp.bfloat16):
    level = levels(rng, dims, cuts, -0.22, 0.18) if cuts else 1.0
    entries = jax.random.normal(rng, dims, jnp.float32) * scale * level
    return jnp.minimum(jnp.maximum(entries, -reach), reach).astype(kind)


def setup_inputs(seed: int = 0) -> dict:
    keys = jax.random.split(jax.random.key(seed), 17)
    return {
        "tokens": normal_values(keys[0], (SEQS, LEN, D), 1.0, 6.0, ((0, 8),)),
        "segments": draw_segments(jax.random.fold_in(keys[16], 71), 0),
        "cotangent": normal_values(keys[2], (SEQS, LEN, D), 1.0, 6.0, ((0, 8),)),
        "inproj": normal_values(keys[3], (D, 3, D), D ** -0.5, 0.21875, ((2, 4),)),
        "querybias": normal_values(keys[4], (D,), 0.3, 4.0, ((0, 4),)),
        "valuebias": normal_values(keys[5], (D,), 0.05, 0.75, ((0, 4),)),
        "outproj": normal_values(keys[6], (D, D), (max(D // 128, 2)) ** -0.5, 2.5, ((0, 4),)),
        "outbias": normal_values(keys[7], (D,), 0.5, 6.0),
        "gainone": jnp.clip(1.0 + 0.15 * jax.random.normal(keys[8], (D,), jnp.float32), 0.25, 1.75).astype(jnp.bfloat16),
        "shiftone": normal_values(keys[9], (D,), 0.3, 4.0),
        "gaintwo": jnp.clip(1.0 + 0.15 * jax.random.normal(keys[10], (D,), jnp.float32), 0.25, 1.75).astype(jnp.bfloat16),
        "shifttwo": normal_values(keys[11], (D,), 0.3, 4.0),
        "expand": normal_values(keys[12], (D, FF), D ** -0.5, 0.21875, ((1, 4),)),
        "expandbias": normal_values(keys[13], (FF,), 0.5, 6.0, ((0, 4),)),
        "contract": normal_values(keys[14], (FF, D), FF ** -0.5, 0.109375, ((0, 4),)),
        "contractbias": normal_values(keys[15], (D,), 0.5, 6.0),
    }


@jax.custom_vjp
def low(v):
    return lax.optimization_barrier(v.astype(jnp.bfloat16)).astype(jnp.float32)

@jax.custom_vjp
def low_back(v):
    return v

def low_keep(v):
    return (low(v), None)

def low_pass(kept, grad):
    return (grad,)

def back_keep(v):
    return (v, None)

def back_low(kept, grad):
    return (low(grad),)
low.defvjp(low_keep, low_pass)
low_back.defvjp(back_keep, back_low)
EPSILON = 1e-06
SCORE_SCALE = 0.125
MASKED_SCORE = -1e+30
HIGHEST = lax.Precision.HIGHEST

def layer_norm(values, gain, shift):
    row_mean = lax.optimization_barrier(jnp.mean(values, -1, keepdims=True))
    centred = values - row_mean
    spread = lax.optimization_barrier(jnp.mean(centred * centred, -1, keepdims=True))
    return centred * lax.rsqrt(spread + EPSILON) * gain + shift

def forward(inputs, segment, params):
    inproj, querybias, valuebias, outproj, outbias, gainone, shiftone, gaintwo, shifttwo, expand, expandbias, contract, contractbias = params
    normed = low(layer_norm(inputs, gainone, shiftone))
    bias_rows = jnp.stack([querybias, jnp.zeros_like(querybias), valuebias])
    projected = jnp.einsum('td,dcf->tcf', normed, inproj, precision=HIGHEST) + bias_rows
    projected = low(low_back(projected))
    queries = projected[:, 0].reshape(LEN, H, HD)
    key_rows = projected[:, 1].reshape(LEN, H, HD)
    value_rows = projected[:, 2].reshape(LEN, H, HD)
    scores = jnp.einsum('qhd,khd->hqk', queries, key_rows, precision=HIGHEST) * SCORE_SCALE
    scores = low_back(scores)
    same_tile = segment[:, None] == segment[None, :]
    scores = jnp.where(same_tile[None], scores, MASKED_SCORE)
    attn_probs = low(jax.nn.softmax(scores, axis=-1))
    head_out = jnp.einsum('hqk,khd->qhd', attn_probs, value_rows, precision=HIGHEST)
    head_out = low(low_back(head_out)).reshape(LEN, D)
    per_group = D // N_TENSOR
    partials = jnp.einsum('qgc,gco->gqo', head_out.reshape(LEN, N_TENSOR, per_group), outproj.reshape(N_TENSOR, per_group, D), precision=HIGHEST)
    middle = inputs + low_back(lax.optimization_barrier(jnp.sum(low(partials), 0)) + outbias)
    second = low(layer_norm(middle, gaintwo, shifttwo))
    hidden = jnp.dot(second, expand, precision=HIGHEST, preferred_element_type=jnp.float32) + expandbias
    hidden = low_back(hidden)
    active = low(jax.nn.gelu(hidden, approximate=False))
    hidden_group = FF // N_TENSOR
    partials_two = jnp.einsum('qgc,gco->gqo', active.reshape(LEN, N_TENSOR, hidden_group), contract.reshape(N_TENSOR, hidden_group, D), precision=HIGHEST)
    return middle + low_back(lax.optimization_barrier(jnp.sum(low(partials_two), 0)) + contractbias)

def reference(tokens, segments, cotangent, inproj, querybias, valuebias, outproj, outbias, gainone, shiftone, gaintwo, shifttwo, expand, expandbias, contract, contractbias):
    params = tuple((weight.astype(jnp.float32) for weight in (inproj, querybias, valuebias, outproj, outbias, gainone, shiftone, gaintwo, shifttwo, expand, expandbias, contract, contractbias)))

    def one_sequence(totals, sequence):
        token_rows, segment, upstream = sequence
        inputs = token_rows.astype(jnp.float32)
        upstream = jnp.where((segment > 0)[:, None], upstream.astype(jnp.float32), 0.0)
        result, pullback = jax.vjp(lambda first_arg, second_arg: forward(first_arg, segment, second_arg), inputs, params)
        grad_in, grad_params = pullback(upstream)
        totals = jax.tree.map(jnp.add, totals, grad_params)
        return (totals, (result.astype(jnp.bfloat16), grad_in.astype(jnp.bfloat16)))
    starting = jax.tree.map(jnp.zeros_like, params)
    totals, (layer_out, token_grad) = lax.scan(one_sequence, starting, (tokens, segments, cotangent))
    return (layer_out, token_grad, totals[0], totals[1], totals[2], totals[3], totals[4], totals[5], totals[6], totals[7], totals[8], totals[9], totals[10], totals[11], totals[12])
```

```python
import functools

import jax
import jax.numpy as jnp
from jax import lax
from jax.experimental import pallas as pl
from jax.experimental.pallas import tpu as pltpu
from jax.sharding import PartitionSpec as P

BF = jnp.bfloat16
F32 = jnp.float32
EPSILON = 1e-06
LOG2E = 1.4426950408889634
ROOT_HALF = 0.7071067811865476
INV_ROOT_TWO_PI = 0.3989422804014327
MASKED = -1e30
MESH = pl.DeviceIdType.MESH
RT = 192
NZ = 4
OUT_BIAS, GAIN_ONE, SHIFT_ONE, GAIN_TWO, SHIFT_TWO, CONTRACT_BIAS = range(6)
ATT, EXP, CON = range(3)


def nt(a, b):
    return lax.dot_general(a, b, (((1,), (1,)), ((), ())), preferred_element_type=F32)


def nn(a, b):
    return lax.dot_general(a, b, (((1,), (0,)), ((), ())), preferred_element_type=F32)


def tn(a, b):
    return lax.dot_general(a, b, (((0,), (0,)), ((), ())), preferred_element_type=F32)


def at128(i):
    return pl.ds(pl.multiple_of(i * 128, 128), 128)


def at256(i):
    return pl.ds(pl.multiple_of(i * 256, 256), 256)


def rows(i):
    return pl.ds(pl.multiple_of(i * RT, RT), RT)


def loop(n, f):
    def body(i, carry):
        f(i)
        return carry

    lax.fori_loop(0, n, body, 0)


def standardize(v):
    mu = jnp.mean(v, -1, keepdims=True)
    c = v - mu
    inv = lax.rsqrt(jnp.mean(c * c, -1, keepdims=True) + EPSILON)
    return c * inv, inv


def norm_back(z, unit, inv, gain):
    s = z * gain
    a = jnp.mean(s, -1, keepdims=True)
    b = jnp.mean(s * unit, -1, keepdims=True)
    return inv * (s - a - unit * b)


def head_lanes(shape, h):
    lane = lax.broadcasted_iota(jnp.int32, shape, 1)
    return (lane < 64) if h == 0 else (lane >= 64)


class Bag:
    pass


def make_mask(S):
    def f(i):
        S.mask[rows(i), :] = jnp.where(S.seg_col[rows(i), 0:1] == S.seg_row[0:1, :], 0.0, MASKED)

    loop(S.nrt, f)


def first_norm(S):
    def f(i):
        u, _ = standardize(S.x[rows(i), :].astype(F32))
        S.normed[rows(i), :] = (
            u * S.vec[GAIN_ONE : GAIN_ONE + 1, :] + S.vec[SHIFT_ONE : SHIFT_ONE + 1, :]
        ).astype(BF)

    loop(S.nrt, f)


def head_rows(S, c, j):
    w = S.d // NZ
    out = []
    lo = 256 * j
    while lo < 256 * (j + 1):
        r = lo // w
        n = min(256 * (j + 1), (r + 1) * w) - lo
        out.append((r, c * w + (lo - r * w), n))
        lo += n
    return out


def project(S):
    bias_q = S.bias[0, 0:1, :] + S.bias[1, 0:1, :] + S.bias[2, 0:1, :] + S.bias[3, 0:1, :]
    bias_v = S.bias[0, 1:2, :] + S.bias[1, 1:2, :] + S.bias[2, 1:2, :] + S.bias[3, 1:2, :]
    S.qkv_bias[0:1, :] = bias_q
    S.qkv_bias[1:2, :] = jnp.zeros_like(bias_q)
    S.qkv_bias[2:3, :] = bias_v

    def f(c):
        for j in range(S.d // 256):
            w = jnp.concatenate(
                [S.w[ATT][r, pl.ds(pl.multiple_of(c * (S.d // NZ), 64) + (o), n), :] for r, o, n in head_rows(S, 0, j)], 0
            )
            y = nt(S.normed[...], w) + S.qkv_bias[pl.ds(c, 1), 256 * j : 256 * j + 256]
            S.proj[:, pl.ds(pl.multiple_of(c * S.d + 256 * j, 256), 256)] = y.astype(BF)

    loop(3, f)


def attend_pair(S, p):
    np_ = S.d // 128
    k2 = S.proj[:, at128(np_ + p)]
    v2 = S.proj[:, at128(2 * np_ + p)]

    def f(i):
        q2 = S.proj[rows(i), at128(p)]
        os = []
        for h in (0, 1):
            qm = jnp.where(head_lanes(q2.shape, h), q2, jnp.zeros_like(q2))
            s = nt(qm, k2) * (0.125 * LOG2E) + S.mask[rows(i), :]
            e = jnp.exp2(s - jnp.max(s, -1, keepdims=True))
            pr = (e * (1.0 / jnp.sum(e, -1, keepdims=True))).astype(BF)
            S.probs[2 * p + h, rows(i), :] = pr
            os.append(nn(pr, v2))
        S.heads[rows(i), at128(p)] = jnp.where(head_lanes(os[0].shape, 0), os[0], os[1]).astype(BF)

    loop(S.nrt, f)


def out_matrix(S):
    w = S.d // NZ
    return jnp.concatenate([S.w[ATT][r, 3 * w : 4 * w, :] for r in range(NZ)], 0)


def attend_out(S):
    def f(i):
        m = (
            S.x[rows(i), :].astype(F32)
            + nn(S.heads[rows(i), :], out_matrix(S))
            + S.vec[OUT_BIAS : OUT_BIAS + 1, :]
        )
        S.middle[rows(i), :] = m
        u, _ = standardize(m)
        S.second[rows(i), :] = (
            u * S.vec[GAIN_TWO : GAIN_TWO + 1, :] + S.vec[SHIFT_TWO : SHIFT_TWO + 1, :]
        ).astype(BF)

    loop(S.nrt, f)


def expand_up(S):
    def f(r):
        for j in range(S.d // 256):
            h = nn(S.second[...], S.w[EXP][r, :, 256 * j : 256 * j + 256])
            h = h + S.bias[r, 2:3, 256 * j : 256 * j + 256]
            cdf = 0.5 + 0.5 * lax.erf(h * ROOT_HALF)
            c = pl.ds(pl.multiple_of(r * S.d + 256 * j, 256), 256)
            S.active[:, c] = (h * cdf).astype(BF)
            S.slope[:, c] = (cdf + h * jnp.exp2(h * h * (-0.5 * LOG2E)) * INV_ROOT_TWO_PI).astype(BF)

    loop(NZ, f)


def contract_down(S):
    def f(i):
        a = S.middle[rows(i), :] + S.vec[CONTRACT_BIAS : CONTRACT_BIAS + 1, :]
        for r in range(NZ):
            a = a + nn(S.active[rows(i), S.d * r : S.d * r + S.d], S.w[CON][r])
        S.layer[rows(i), :] = a.astype(BF)

    loop(S.nrt, f)


def mask_upstream(S):
    S.small[...] = jnp.zeros_like(S.small)

    def f(i):
        g = jnp.where(S.seg_col[rows(i), 0:1] > 0, S.up[rows(i), :].astype(F32), 0.0)
        S.up[rows(i), :] = g.astype(BF)
        S.small[4:5, :] += jnp.sum(g, 0, keepdims=True)

    loop(S.nrt, f)


def hidden_back(S):
    def f(r):
        for j in range(S.d // 256):
            c = pl.ds(pl.multiple_of(r * S.d + 256 * j, 256), 256)
            ga = nt(S.up[...], S.w[CON][r, 256 * j : 256 * j + 256, :])
            gh = (ga * S.slope[:, c].astype(F32)).astype(BF)
            S.slope[:, c] = gh
            S.small[pl.ds(r, 1), 256 * j : 256 * j + 256] = jnp.sum(gh.astype(F32), 0, keepdims=True)

    loop(NZ, f)


def contract_grad(S):
    def f(r):
        for j in range(S.d // 256):
            c = pl.ds(pl.multiple_of(r * S.d + 256 * j, 256), 256)
            S.w[CON][r, 256 * j : 256 * j + 256, :] = tn(S.active[:, c], S.up[...]).astype(BF)

    loop(NZ, f)


def second_back(S):
    def f(i):
        gs = nt(S.slope[rows(i), 0 : S.d], S.w[EXP][0])
        for r in range(1, NZ):
            gs = gs + nt(S.slope[rows(i), S.d * r : S.d * r + S.d], S.w[EXP][r])
        u, inv = standardize(S.middle[rows(i), :])
        gm = S.up[rows(i), :].astype(F32) + norm_back(gs, u, inv, S.vec[GAIN_TWO : GAIN_TWO + 1, :])
        S.middle[rows(i), :] = gm
        gb = gm.astype(BF)
        S.branch[rows(i), :] = gb
        S.small[8:9, :] += jnp.sum(gs * u, 0, keepdims=True)
        S.small[9:10, :] += jnp.sum(gs, 0, keepdims=True)
        S.small[5:6, :] += jnp.sum(gb.astype(F32), 0, keepdims=True)

    loop(S.nrt, f)


def expand_grad(S):
    S.flipped[...] = S.second[...].T

    def f(r):
        for j in range(S.d // 256):
            c = pl.ds(pl.multiple_of(r * S.d + 256 * j, 256), 256)
            S.w[EXP][r, :, 256 * j : 256 * j + 256] = nn(S.flipped[...], S.slope[:, c]).astype(BF)

    loop(NZ, f)


def heads_back(S):
    def f(i):
        S.gheads[rows(i), :] = nt(S.branch[rows(i), :], out_matrix(S)).astype(BF)

    loop(S.nrt, f)


def store_head_rows(S, c, j, v):
    at = 0
    for r, o, n in head_rows(S, c, j):
        S.w[ATT][r, o : o + n, :] = v[at : at + n, :]
        at += n


def outproj_grad(S):
    for j in range(S.d // 256):
        v = tn(S.heads[:, 256 * j : 256 * j + 256], S.branch[...]).astype(BF)
        store_head_rows(S, 3, j, v)


def attend_back_pair(S, p):
    np_ = S.d // 128
    k2 = S.proj[:, at128(np_ + p)]
    v2 = S.proj[:, at128(2 * np_ + p)]
    S.acc[...] = jnp.zeros_like(S.acc)

    def f(i):
        q2 = S.proj[rows(i), at128(p)]
        g2 = S.gheads[rows(i), at128(p)]
        od = g2.astype(F32) * S.heads[rows(i), at128(p)].astype(F32)
        dq, dk, dv = [], [], []
        for h in (0, 1):
            hm = head_lanes(q2.shape, h)
            gm = jnp.where(hm, g2, jnp.zeros_like(g2))
            dot_sum = jnp.sum(jnp.where(hm, od, 0.0), -1, keepdims=True)
            pr = S.probs[2 * p + h, rows(i), :]
            ds = (pr.astype(F32) * (nt(gm, v2) - dot_sum)).astype(BF)
            dq.append(nn(ds, k2))
            dk.append(tn(ds, q2))
            dv.append(tn(pr, g2))
        S.proj[rows(i), at128(p)] = (
            jnp.where(head_lanes(dq[0].shape, 0), dq[0], dq[1]) * 0.125
        ).astype(BF)
        hm = head_lanes(dk[0].shape, 0)
        S.acc[0] += jnp.where(hm, dk[0], dk[1])
        S.acc[1] += jnp.where(hm, dv[0], dv[1])

    loop(S.nrt, f)
    S.proj[:, at128(np_ + p)] = (S.acc[0] * 0.125).astype(BF)
    S.proj[:, at128(2 * np_ + p)] = S.acc[1].astype(BF)


def first_back(S):
    w = S.d // NZ

    def f(i):
        gf = None
        for c in range(3):
            m = jnp.concatenate([S.w[ATT][r, c * w : (c + 1) * w, :] for r in range(NZ)], 0)
            y = nn(S.proj[rows(i), c * S.d : (c + 1) * S.d], m)
            gf = y if gf is None else gf + y
        u, inv = standardize(S.x[rows(i), :].astype(F32))
        S.token[rows(i), :] = (
            S.middle[rows(i), :] + norm_back(gf, u, inv, S.vec[GAIN_ONE : GAIN_ONE + 1, :])
        ).astype(BF)
        S.small[6:7, :] += jnp.sum(gf * u, 0, keepdims=True)
        S.small[7:8, :] += jnp.sum(gf, 0, keepdims=True)
        S.small[10:11, :] += jnp.sum(S.proj[rows(i), 0 : S.d].astype(F32), 0, keepdims=True)
        S.small[11:12, :] += jnp.sum(S.proj[rows(i), 2 * S.d : 3 * S.d].astype(F32), 0, keepdims=True)

    loop(S.nrt, f)


def inproj_grad(S):
    for c in range(3):
        for j in range(S.d // 256):
            v = tn(S.proj[:, c * S.d + 256 * j : c * S.d + 256 * j + 256], S.normed[...]).astype(BF)
            store_head_rows(S, c, j, v)


class Links:
    def __init__(self, n_dp):
        self.dp = lax.axis_index("dp")
        self.t = lax.axis_index("tensor")
        self.c = self.dp % 2
        bx = (self.dp // 2) % 2
        by = (self.dp // 4) % 2
        self.b1 = bx + self.c * (by - bx)
        self.b2 = by + self.c * (bx - by)
        self.sib = self.dp + 1 - 2 * self.c
        self.p1 = self.dp + (1 - 2 * self.b1) * (2 + 2 * self.c)
        self.p2 = self.dp + (1 - 2 * self.b2) * (4 - 2 * self.c)
        self.more = []
        step = 8
        while step < n_dp:
            self.more.append(self.dp + (1 - 2 * ((self.dp // step) % 2)) * step)
            step *= 2

    def peer(self, r):
        return (self.t + r) % NZ

    def to(self, dp=None, t=None):
        return {"dp": self.dp if dp is None else dp, "tensor": self.t if t is None else t}


def remote(src, dst, ssem, rsem, to):
    return pltpu.make_async_remote_copy(
        src_ref=src, dst_ref=dst, send_sem=ssem, recv_sem=rsem, device_id=to, device_id_type=MESH
    )


class Gather:
    def __init__(self, S, L, ch):
        d = S.d
        q, h = d // 4, d // 2
        cols = pl.ds(pl.multiple_of(L.c * h, 128), h)
        w = S.w[ch]

        def quarter(k):
            return pl.ds(pl.multiple_of(k * q, 64), q)

        mine = quarter(2 * L.b2 + L.b1)
        near = quarter(2 * L.b2 + 1 - L.b1)
        upper = pl.ds(pl.multiple_of(L.b2 * h, 128), h)
        lower = pl.ds(pl.multiple_of((1 - L.b2) * h, 128), h)
        ss, rs = S.gsend, S.grecv
        src = S.shard[ch]
        self.local = pltpu.make_async_copy(src, w.at[0], S.lsem.at[ch])
        self.z = [
            remote(src.at[mine, cols], w.at[r, mine, cols], ss.at[ch, r - 1], rs.at[ch, r - 1], L.to(t=L.peer(NZ - r)))
            for r in range(1, NZ)
        ]
        far = pl.ds(1, NZ - 1)
        self.one = remote(w.at[far, mine, cols], w.at[far, mine, cols], ss.at[ch, 3], rs.at[ch, 3], L.to(dp=L.p1))
        self.two = remote(w.at[far, upper, cols], w.at[far, upper, cols], ss.at[ch, 4], rs.at[ch, 4], L.to(dp=L.p2))
        self.sib = [
            remote(w.at[far, k, cols], w.at[far, k, cols], ss.at[ch, 5 + i], rs.at[ch, 5 + i], L.to(dp=L.sib))
            for i, k in enumerate((mine, near, lower))
        ]

    def start(self):
        self.local.start()
        for k in self.z:
            k.start()

    def after_z(self):
        for k in self.z:
            k.wait_recv()
        self.one.start()
        self.sib[0].start()

    def after_one(self):
        self.one.wait_recv()
        self.two.start()
        self.sib[1].start()

    def after_two(self):
        self.two.wait_recv()
        self.sib[2].start()

    def finish(self):
        self.local.wait()
        for k in self.sib:
            k.wait_recv()

    def drain(self):
        for k in self.z + [self.one, self.two] + self.sib:
            k.wait_send()


class Reduce:
    def __init__(self, S, L, ch):
        d = S.d
        q, h = d // 4, d // 2
        self.S, self.L, self.ch, self.q, self.h = S, L, ch, q, h
        w = S.w[ch]
        self.w = w
        self.c0 = pl.multiple_of(L.c * h, 128)
        cols = pl.ds(self.c0, h)
        other = pl.ds(pl.multiple_of((1 - L.c) * h, 128), h)
        self.cols = cols

        def quarter(k):
            return pl.ds(pl.multiple_of(k * q, 64), q)

        self.q0 = pl.multiple_of((2 * L.b2 + L.b1) * q, 64)
        mine = pl.ds(self.q0, q)
        near = quarter(2 * L.b2 + 1 - L.b1)
        self.u0 = pl.multiple_of(L.b2 * h, 128)
        upper = pl.ds(self.u0, h)
        lower = pl.ds(pl.multiple_of((1 - L.b2) * h, 128), h)
        ss, rs = S.rsend, S.rrecv
        out = S.gout.at[ch]
        self.core = remote(w.at[:, :, other], S.r1.at[ch], ss.at[ch, 0], rs.at[ch, 0], L.to(dp=L.sib))
        self.two = remote(w.at[:, lower, cols], S.r2.at[ch], ss.at[ch, 1], rs.at[ch, 1], L.to(dp=L.p2))
        self.one = remote(w.at[:, near, cols], S.r3.at[ch], ss.at[ch, 2], rs.at[ch, 2], L.to(dp=L.p1))
        self.z = [
            remote(w.at[r, mine, cols], S.r4.at[ch, NZ - 1 - r], ss.at[ch, 2 + r], rs.at[ch, 6 - r], L.to(t=L.peer(r)))
            for r in range(1, NZ)
        ]
        self.more = [
            remote(S.r6.at[ch, i], S.r5.at[ch, i], ss.at[ch, 11 + i], rs.at[ch, 11 + i], L.to(dp=m))
            for i, m in enumerate(L.more)
        ]
        own = w.at[0, mine, cols]
        self.keep = pltpu.make_async_copy(own, out.at[mine, cols], S.lsem.at[3 + ch])
        self.back_one = remote(own, out.at[mine, cols], ss.at[ch, 6], rs.at[ch, 6], L.to(dp=L.p1))
        self.back_two = remote(out.at[upper, cols], out.at[upper, cols], ss.at[ch, 7], rs.at[ch, 7], L.to(dp=L.p2))
        self.back_sib = [
            remote(own, out.at[mine, cols], ss.at[ch, 8], rs.at[ch, 8], L.to(dp=L.sib)),
            remote(out.at[near, cols], out.at[near, cols], ss.at[ch, 9], rs.at[ch, 9], L.to(dp=L.sib)),
            remote(out.at[lower, cols], out.at[lower, cols], ss.at[ch, 10], rs.at[ch, 10], L.to(dp=L.sib)),
        ]

    def start(self):
        self.core.start()

    def add(self, src, first, count):
        w, cols = self.w, self.cols
        step = self.q

        def f(i):
            r, k = i // (count // step), i % (count // step)
            at = pl.ds(first + pl.multiple_of(k * step, 64), step)
            got = src[r, pl.ds(pl.multiple_of(k * step, 64), step), :].astype(F32)
            w[r, at, cols] = (w[r, at, cols].astype(F32) + got).astype(BF)

        loop(NZ * (count // step), f)

    def after_core(self):
        self.core.wait()
        self.add(self.S.r1.at[self.ch], 0, 2 * self.h)
        self.two.start()

    def after_two(self):
        self.two.wait()
        self.add(self.S.r2.at[self.ch], self.u0, self.h)
        self.one.start()

    def after_one(self):
        self.one.wait()
        self.add(self.S.r3.at[self.ch], self.q0, self.q)
        for k in self.z:
            k.start()

    def after_z(self):
        S, w = self.S, self.w
        for k in self.z:
            k.wait()
        mine = pl.ds(self.q0, self.q)
        v = w[0, mine, self.cols].astype(F32)
        for k in range(NZ - 1):
            v = v + S.r4[self.ch, k].astype(F32)
        for i, k in enumerate(self.more):
            S.r6[self.ch, i] = v.astype(BF)
            k.start()
            k.wait()
            v = S.r6[self.ch, i].astype(F32) + S.r5[self.ch, i].astype(F32)
        w[0, mine, self.cols] = v.astype(BF)
        self.keep.start()
        self.back_one.start()
        self.back_sib[0].start()

    def after_back_one(self):
        self.keep.wait()
        self.back_one.wait()
        self.back_two.start()
        self.back_sib[1].start()

    def after_back_two(self):
        self.back_two.wait()
        self.back_sib[2].start()

    def finish(self):
        for k in self.back_sib:
            k.wait()


class Spread:
    def __init__(self, S, L, k, own, out):
        self.t = L.t
        ss, rs = S.osend, S.orecv
        right, left = L.to(t=(L.t + 1) % NZ), L.to(t=(L.t + NZ - 1) % NZ)

        def block(j):
            return out.at[(L.t + j + NZ) % NZ]

        self.keep = pltpu.make_async_copy(own, out.at[L.t], S.lsem.at[6 + k])
        self.right = [remote(own if i == 0 else block(-i), block(-i), ss.at[k, i], rs.at[k, i], right) for i in range(NZ - 1)]
        self.left = [
            remote(own if i == 0 else block(i), block(i), ss.at[k, 3 + i], rs.at[k, 3 + i], left) for i in range(NZ - 1)
        ]

    def start(self):
        self.keep.start()
        self.send(0)

    def send(self, i):
        @pl.when((self.t >= i) & (self.t < NZ - 1))
        def _():
            self.right[i].start()

        @pl.when((self.t <= NZ - 1 - i) & (self.t > 0))
        def _():
            self.left[i].start()

    def arrive(self, i):
        @pl.when(self.t >= i + 1)
        def _():
            self.right[i].wait_recv()

        @pl.when(self.t <= NZ - 2 - i)
        def _():
            self.left[i].wait_recv()

    def forward(self, i):
        self.arrive(i - 1)
        self.send(i)

    def finish(self):
        self.keep.wait()
        self.arrive(NZ - 2)
        for i in range(NZ - 1):

            @pl.when((self.t >= i) & (self.t < NZ - 1))
            def _():
                self.right[i].wait_send()

            @pl.when((self.t <= NZ - 1 - i) & (self.t > 0))
            def _():
                self.left[i].wait_send()


class SmallSum:
    def __init__(self, S, L):
        self.S = S
        ss, rs = S.ssend, S.srecv
        partners = [L.sib, L.p1, L.p2] + L.more
        self.rounds = [
            remote(S.small_out.at[i], S.small_in.at[i], ss.at[i], rs.at[i], L.to(dp=p)) for i, p in enumerate(partners)
        ]
        n = len(partners)
        self.keep = pltpu.make_async_copy(S.small, S.sums.at[L.t], S.lsem.at[8])
        self.z = [
            remote(S.small, S.sums.at[L.t], ss.at[n + r - 1], rs.at[n + NZ - 1 - r], L.to(t=L.peer(r)))
            for r in range(1, NZ)
        ]

    def start(self, i):
        self.S.small_out[i] = self.S.small[...]
        self.rounds[i].start()

    def after(self, i):
        self.rounds[i].wait()
        self.S.small[...] += self.S.small_in[i]
        if i + 1 < len(self.rounds):
            self.start(i + 1)
        else:
            self.keep.start()
            for k in self.z:
                k.start()

    def finish(self):
        self.keep.wait()
        for k in self.z:
            k.wait()


NAMES_IN = ("tokens", "cot", "seg_col", "seg_row", "wa", "we", "wc", "bias_in", "vec")
NAMES_OUT = ("layers", "token_grads", "gout", "sums")


def layer_kernel(n_dp, names, *refs):
    S = Bag()
    for n, r in zip(names, refs):
        setattr(S, n, r)
    S.t, S.d = S.x.shape
    S.nrt = S.t // RT
    S.w = [S.wbuf.at[0], S.wbuf.at[1], S.wbuf.at[2]]
    S.shard = [S.wa, S.we, S.wc]
    L = Links(n_dp)

    barrier = pltpu.get_barrier_semaphore()
    partners = [L.to(dp=p) for p in [L.sib, L.p1, L.p2] + L.more] + [L.to(t=L.peer(r)) for r in range(1, NZ)]
    for p in partners:
        pl.semaphore_signal(barrier, inc=1, device_id=p, device_id_type=MESH)
    load_x = pltpu.make_async_copy(S.tokens.at[L.t], S.x, S.lsem.at[9])
    load_up = pltpu.make_async_copy(S.cot.at[L.t], S.up, S.lsem.at[10])
    load_x.start()
    load_up.start()
    pl.semaphore_wait(barrier, len(partners))

    bias = [
        remote(S.bias_in.at[r], S.bias.at[r], S.bsend.at[r - 1], S.brecv.at[r - 1], L.to(t=L.peer(NZ - r)))
        for r in range(1, NZ)
    ]
    G = [Gather(S, L, ch) for ch in range(3)]
    R = [Reduce(S, L, ch) for ch in range(3)]
    layers = Spread(S, L, 0, S.layer, S.layers)
    tokens = Spread(S, L, 1, S.token, S.token_grads)
    small = SmallSum(S, L)

    G[ATT].start()
    for k in bias:
        k.start()
    G[EXP].start()
    G[CON].start()
    S.bias[0] = S.bias_in[0]
    make_mask(S)
    load_x.wait()
    first_norm(S)

    G[ATT].after_z()
    G[ATT].after_one()
    G[EXP].after_z()
    G[ATT].after_two()
    for k in bias:
        k.wait()
    G[ATT].finish()
    project(S)

    def pair(p):
        attend_pair(S, p)
        for at, step in enumerate(
            (G[EXP].after_one, G[CON].after_z, G[EXP].after_two, G[CON].after_one, G[CON].after_two)
        ):
            pl.when(p == at)(step)

    loop(S.d // 128, pair)
    attend_out(S)
    G[EXP].finish()
    expand_up(S)
    G[CON].finish()
    contract_down(S)
    layers.start()
    for g in G:
        g.drain()

    load_up.wait()
    mask_upstream(S)
    hidden_back(S)
    contract_grad(S)
    R[CON].start()
    second_back(S)
    R[CON].after_core()
    expand_grad(S)
    R[EXP].start()
    layers.forward(1)
    heads_back(S)
    outproj_grad(S)
    R[EXP].after_core()

    def pair_back(p):
        attend_back_pair(S, p)
        for at, step in enumerate(
            (R[CON].after_two, lambda: layers.forward(2), R[EXP].after_two, R[CON].after_one, R[EXP].after_one, R[CON].after_z)
        ):
            pl.when(p == at)(step)

    loop(S.d // 128, pair_back)
    first_back(S)
    tokens.start()
    small.start(0)
    inproj_grad(S)
    R[ATT].start()
    R[CON].after_back_one()
    R[EXP].after_z()
    small.after(0)
    R[ATT].after_core()
    R[CON].after_back_two()
    R[EXP].after_back_one()
    small.after(1)
    tokens.forward(1)
    R[ATT].after_two()
    small.after(2)
    for i in range(3, 3 + len(L.more)):
        small.after(i)
    R[EXP].after_back_two()
    R[ATT].after_one()
    layers.finish()
    R[ATT].after_z()
    tokens.forward(2)
    R[ATT].after_back_one()
    R[ATT].after_back_two()
    for r in R:
        r.finish()
    small.finish()
    tokens.finish()


def run_layer(n_dp, tokens, cot, seg_col, seg_row, wa, we, wc, bias_in, vec):
    _, t, d = tokens.shape
    hidden = we.shape[1] * NZ
    more = max(n_dp.bit_length() - 1 - 3, 0)
    spare = max(more, 1)
    any_, vmem = pl.BlockSpec(memory_space=pl.ANY), pl.BlockSpec(memory_space=pltpu.VMEM)
    V, DMA = pltpu.VMEM, pltpu.SemaphoreType.DMA
    scratch = dict(
        x=V((t, d), BF),
        up=V((t, d), BF),
        normed=V((t, d), BF),
        proj=V((t, 3 * d), BF),
        probs=V((d // 64, t, t), BF),
        heads=V((t, d), BF),
        middle=V((t, d), F32),
        second=V((t, d), BF),
        active=V((t, hidden), BF),
        slope=V((t, hidden), BF),
        branch=V((t, d), BF),
        gheads=V((t, d), BF),
        flipped=V((d, t), BF),
        acc=V((2, t, 128), F32),
        mask=V((t, t), F32),
        layer=V((t, d), BF),
        token=V((t, d), BF),
        wbuf=V((3, NZ, d, d), BF),
        bias=V((NZ, 8, d), F32),
        qkv_bias=V((8, d), F32),
        small=V((16, d), F32),
        small_in=V((3 + more, 16, d), F32),
        small_out=V((3 + more, 16, d), F32),
        r1=V((3, NZ, d, d // 2), BF),
        r2=V((3, NZ, d // 2, d // 2), BF),
        r3=V((3, NZ, d // 4, d // 2), BF),
        r4=V((3, NZ - 1, d // 4, d // 2), BF),
        r5=V((3, spare, d // 4, d // 2), BF),
        r6=V((3, spare, d // 4, d // 2), BF),
        lsem=DMA((11,)),
        gsend=DMA((3, 8)),
        grecv=DMA((3, 8)),
        rsend=DMA((3, 11 + spare)),
        rrecv=DMA((3, 11 + spare)),
        osend=DMA((2, 6)),
        orecv=DMA((2, 6)),
        ssend=DMA((6 + more,)),
        srecv=DMA((6 + more,)),
        bsend=DMA((3,)),
        brecv=DMA((3,)),
    )
    names = NAMES_IN + NAMES_OUT + tuple(scratch)
    out_shape = [
        jax.ShapeDtypeStruct((NZ, t, d), BF),
        jax.ShapeDtypeStruct((NZ, t, d), BF),
        jax.ShapeDtypeStruct((3, d, d), BF),
        jax.ShapeDtypeStruct((NZ, 16, d), F32),
    ]
    return pl.pallas_call(
        functools.partial(layer_kernel, n_dp, names),
        out_shape=out_shape,
        in_specs=[any_, any_, vmem, vmem, any_, any_, any_, vmem, vmem],
        out_specs=[any_] * 4,
        scratch_shapes=list(scratch.values()),
        compiler_params=pltpu.CompilerParams(
            collective_id=0, has_side_effects=True, vmem_limit_bytes=63 << 20
        ),
        name="layer",
    )(tokens, cot, seg_col, seg_row, wa, we, wc, bias_in, vec)


def local(
    n_dp,
    tokens,
    segments,
    cotangent,
    inproj,
    querybias,
    valuebias,
    outproj,
    outbias,
    gainone,
    shiftone,
    gaintwo,
    shifttwo,
    expand,
    expandbias,
    contract,
    contractbias,
):
    _, t, d = tokens.shape
    w = d // NZ
    me = lax.axis_index("tensor")
    seg = lax.dynamic_slice_in_dim(segments, me, 1, 0)
    seg_row = jnp.broadcast_to(seg, (8, t))
    seg_col = jnp.broadcast_to(seg.reshape(t, 1), (t, 128))
    wa = jnp.concatenate([inproj.transpose(1, 2, 0).reshape(3 * w, d), outproj], 0)

    def placed(v):
        return jnp.stack([jnp.pad(v.astype(F32), (w * r, d - w * (r + 1))) for r in range(NZ)])

    eb = jnp.broadcast_to(expandbias.astype(F32), (NZ, d))
    bias_in = jnp.stack([placed(querybias), placed(valuebias), eb] + [jnp.zeros((NZ, d), F32)] * 5, 1)
    vec = jnp.stack([outbias, gainone, shiftone, gaintwo, shifttwo, contractbias, outbias, outbias]).astype(F32)
    layers, token_grads, gout, sums = run_layer(
        n_dp, tokens, cotangent, seg_col, seg_row, wa, expand, contract, bias_in, vec
    )
    total = sums[0] + sums[1] + sums[2] + sums[3]
    pick = (jnp.arange(NZ)[None, :] == (me - jnp.arange(NZ)[:, None]) % NZ).astype(F32)[:, :, None]
    eb_grad = jnp.sum(sums[:, 0:NZ] * pick, (0, 1))
    qb_grad = jnp.sum(sums[:, 10].reshape(NZ, NZ, w) * pick, (0, 1))
    vb_grad = jnp.sum(sums[:, 11].reshape(NZ, NZ, w) * pick, (0, 1))
    ga = gout[ATT].astype(F32)
    return (
        layers,
        token_grads,
        ga[: 3 * w].reshape(3, w, d).transpose(2, 0, 1),
        qb_grad,
        vb_grad,
        ga[3 * w :],
        total[5],
        total[6],
        total[7],
        total[8],
        total[9],
        gout[EXP].astype(F32),
        eb_grad,
        gout[CON].astype(F32),
        total[4],
    )


def solution(mesh):
    in_specs = (
        P("dp", None, None),
        P("dp", None),
        P("dp", None, None),
        P(None, None, "tensor"),
        P("tensor"),
        P("tensor"),
        P("tensor", None),
        P(),
        P(),
        P(),
        P(),
        P(),
        P(None, "tensor"),
        P("tensor"),
        P("tensor", None),
        P(),
    )
    out_specs = (
        P("dp", None, None),
        P("dp", None, None),
        P(None, None, "tensor"),
        P("tensor"),
        P("tensor"),
        P("tensor", None),
        P(),
        P(),
        P(),
        P(),
        P(),
        P(None, "tensor"),
        P("tensor"),
        P("tensor", None),
        P(),
    )
    return jax.shard_map(
        functools.partial(local, mesh.shape["dp"]),
        mesh=mesh,
        in_specs=in_specs,
        out_specs=out_specs,
        check_vma=False,
    )
```

```python
import functools

import jax
import jax.numpy as jnp
from jax import lax
from jax.experimental import pallas as pl
from jax.experimental.pallas import tpu as pltpu
from jax.sharding import PartitionSpec as P

BF = jnp.bfloat16
F32 = jnp.float32
EPSILON = 1e-06
LOG2E = 1.4426950408889634
ROOT_HALF = 0.7071067811865476
INV_ROOT_TWO_PI = 0.3989422804014327
MESH = pl.DeviceIdType.MESH
RT = 192
APART = 2.0**100
NZ = 4
OUT_BIAS, GAIN_ONE, SHIFT_ONE, GAIN_TWO, SHIFT_TWO, CONTRACT_BIAS = range(6)
ATT, EXP, CON = range(3)


def nt(a, b):
    return lax.dot_general(a, b, (((1,), (1,)), ((), ())), preferred_element_type=F32)


def nn(a, b):
    return lax.dot_general(a, b, (((1,), (0,)), ((), ())), preferred_element_type=F32)


def tn(a, b):
    return lax.dot_general(a, b, (((0,), (0,)), ((), ())), preferred_element_type=F32)


def at128(i):
    return pl.ds(pl.multiple_of(i * 128, 128), 128)


def at256(i):
    return pl.ds(pl.multiple_of(i * 256, 256), 256)


def rows(i):
    return pl.ds(pl.multiple_of(i * RT, RT), RT)


def loop(n, f):
    def body(i, carry):
        f(i)
        return carry

    lax.fori_loop(0, n, body, 0)


def standardize(v):
    mu = jnp.mean(v, -1, keepdims=True)
    c = v - mu
    inv = lax.rsqrt(jnp.mean(c * c, -1, keepdims=True) + EPSILON)
    return c * inv, inv


def norm_back(z, unit, inv, gain):
    s = z * gain
    a = jnp.mean(s, -1, keepdims=True)
    b = jnp.mean(s * unit, -1, keepdims=True)
    return inv * (s - a - unit * b)


def head_lanes(shape, h):
    lane = lax.broadcasted_iota(jnp.int32, shape, 1)
    return (lane < 64) if h == 0 else (lane >= 64)


class Bag:
    pass


def segment_column(S, t):
    row = S.segments[pl.ds(t, 1), :].astype(F32)
    S.seg_col[...] = jnp.broadcast_to(row, (128, S.t)).T


def segment_tables(S, t):
    segment_column(S, t)
    lane = lax.broadcasted_iota(jnp.int32, (S.t, 128), 1)
    ids = S.seg_col[...].astype(jnp.int32)
    for h in (0, 1):
        at = lane - (64 if h == 0 else 0)
        same = at == ids
        S.seg_q[h][...] = jnp.where(same, 1.0, 0.0).astype(BF)
        S.seg_k[h][...] = jnp.where((at >= 0) & (at < 8) & (~same), -APART, 0.0).astype(BF)


def first_norm(S, B):
    u, _ = standardize(B.x[...].astype(F32))
    B.normed[...] = (
        u * S.vec[GAIN_ONE : GAIN_ONE + 1, :] + S.vec[SHIFT_ONE : SHIFT_ONE + 1, :]
    ).astype(BF)


def set_bias(S):
    placed = S.bias[0]
    for r in range(1, NZ):
        placed = placed + pltpu.roll(S.bias[r], r * (S.d // NZ), 1)
    S.qkv_bias[...] = placed


def part_matrix(S, B, c):
    w = S.d // NZ
    return jnp.concatenate([B.weight(ATT, r)[c * w : (c + 1) * w, :] for r in range(NZ)], 0)


def project(S, B, c):
    y = nt(B.normed[...], part_matrix(S, B, c)) + S.qkv_bias[c : c + 1, :]
    B.proj[:, c * S.d : (c + 1) * S.d] = y.astype(BF)


def attend_pair(S, B, p):
    n = S.d // 128
    k2 = B.proj[:, at128(n + p)]
    v2 = B.proj[:, at128(2 * n + p)]
    q2 = B.proj[:, at128(p)]
    lane = lax.broadcasted_iota(jnp.int32, (S.t, 128), 1)
    outs, sums = [], []
    for h in (0, 1):
        own = head_lanes(q2.shape, h)
        one = lane == (64 if h == 0 else 0)
        flat = S.keys_t[h]
        flat[...] = jnp.where(own, k2, S.seg_k[h][...]).T
        s = nn(jnp.where(own, q2, S.seg_q[h][...]), flat[...])
        e = jnp.exp2((s - jnp.max(s, -1, keepdims=True)) * (0.125 * LOG2E)).astype(BF)
        if B.keep:
            S.probs(2 * p + h)[...] = e
        o = nn(e, jnp.where(own, v2, jnp.where(one, 1.0, 0.0).astype(BF)))
        at = 64 if h == 0 else 0
        sums.append(1.0 / o[:, at : at + 1])
        outs.append(o)
    first = head_lanes(outs[0].shape, 0)
    scale = jnp.where(first, sums[0], sums[1])
    if B.keep:
        kept = jnp.where(lane == 2 * p, sums[0], S.inv_sum[...])
        S.inv_sum[...] = jnp.where(lane == 2 * p + 1, sums[1], kept)
    B.heads[:, at128(p)] = (jnp.where(first, outs[0], outs[1]) * scale).astype(BF)


def attend_out(S, B):
    m = B.x[...].astype(F32) + nn(B.heads[...], part_matrix(S, B, 3)) + S.vec[OUT_BIAS : OUT_BIAS + 1, :]
    B.middle[...] = m
    u, _ = standardize(m)
    B.second[...] = (
        u * S.vec[GAIN_TWO : GAIN_TWO + 1, :] + S.vec[SHIFT_TWO : SHIFT_TWO + 1, :]
    ).astype(BF)


def expand_up(S, B, done=lambda r: None):
    def g(r):
        w = B.weight(EXP, r)
        for j in range(S.d // 256):
            c = slice(256 * j, 256 * j + 256)
            h = nn(B.second[...], w[:, c]) + S.bias[r, 3:4, c]
            cdf = 0.5 + 0.5 * lax.erf(h * ROOT_HALF)
            B.active(r)[:, c] = (h * cdf).astype(BF)
            if B.keep:
                S.slope(r)[:, c] = (cdf + h * jnp.exp2(h * h * (-0.5 * LOG2E)) * INV_ROOT_TWO_PI).astype(BF)
        done(r)

    loop(NZ, g)


def contract_down(S, B):
    a = (S.layer if B.keep else B.middle)[...].astype(F32) + S.vec[CONTRACT_BIAS : CONTRACT_BIAS + 1, :]
    for r in range(NZ):
        a = a + nn(B.active(r)[...], B.weight(CON, r)[...])
    S.layer[...] = a.astype(BF)


def mask_upstream(S):
    S.small[...] = jnp.zeros_like(S.small)
    g = jnp.where(S.seg_col[:, 0:1] > 0.0, S.up[...].astype(F32), 0.0)
    S.up[...] = g.astype(BF)
    S.small[4:5, :] = jnp.sum(g, 0, keepdims=True)


def hidden_back(S, j, n):
    c = slice(n * j, n * j + n)

    def f(r):
        gh = (nt(S.up[...], S.wbuf[CON, r, c, :]) * S.slope(r)[:, c].astype(F32)).astype(BF)
        S.slope(r)[:, c] = gh
        S.small[pl.ds(r, 1), c] = jnp.sum(gh.astype(F32), 0, keepdims=True)

    loop(NZ, f)


def contract_grad(S, done):
    def f(r):
        S.con_grad[r] = tn(S.own.active(r)[...], S.up[...]).astype(BF)
        done(r)

    loop(NZ, f)


def second_back(S):
    n = S.t // 2
    for k in (8, 9, 5):
        S.small[k : k + 1, :] = jnp.zeros((1, S.d), F32)

    def f(i):
        at = pl.ds(pl.multiple_of(i * n, 32), n)
        gs = nt(S.slope(0)[at, :], S.w[EXP][0])
        for r in range(1, NZ):
            gs = gs + nt(S.slope(r)[at, :], S.w[EXP][r])
        u, inv = standardize(S.middle[at, :])
        gm = S.up[at, :].astype(F32) + norm_back(gs, u, inv, S.vec[GAIN_TWO : GAIN_TWO + 1, :])
        S.middle[at, :] = gm
        gb = gm.astype(BF)
        S.branch[at, :] = gb
        S.small[8:9, :] += jnp.sum(gs * u, 0, keepdims=True)
        S.small[9:10, :] += jnp.sum(gs, 0, keepdims=True)
        S.small[5:6, :] += jnp.sum(gb.astype(F32), 0, keepdims=True)

    loop(2, f)


def expand_grad(S):
    def f(r):
        S.w[EXP][r] = tn(S.second[...], S.slope(r)[...]).astype(BF)

    loop(NZ, f)


def heads_back(S):
    S.gheads[...] = nt(S.branch[...], part_matrix(S, S.own, 3)).astype(BF)


def store_part(S, c, v):
    w = S.d // NZ
    for r in range(NZ):
        S.w[ATT][r, c * w : (c + 1) * w, :] = v[r * w : (r + 1) * w, :]


def outproj_grad(S):
    store_part(S, 3, tn(S.heads[...], S.branch[...]).astype(BF))


def attend_back_pair(S, p):
    n = S.d // 128
    q2 = S.proj[:, at128(p)]
    k2 = S.proj[:, at128(n + p)]
    v2 = S.proj[:, at128(2 * n + p)]
    lane = lax.broadcasted_iota(jnp.int32, (S.t, 128), 1)
    values = S.values_t
    values[...] = v2.T
    kept = S.inv_sum[...]
    scale = [jnp.sum(jnp.where(lane == 2 * p + h, kept, 0.0), -1, keepdims=True) for h in (0, 1)]
    first = head_lanes(q2.shape, 0)
    g2 = (S.gheads[:, at128(p)].astype(F32) * jnp.where(first, scale[0], scale[1])).astype(BF)
    od = g2.astype(F32) * S.heads[:, at128(p)].astype(F32)
    none = jnp.zeros_like(q2)
    dq = None
    for h in (0, 1):
        own = head_lanes(q2.shape, h)
        gm = jnp.where(own, g2, none)
        S.pair_g[h][...] = gm
        S.pair_q[h][...] = jnp.where(own, q2, none)
        dot_sum = jnp.sum(jnp.where(own, od, 0.0), -1, keepdims=True)
        ds = (S.probs(2 * p + h)[...].astype(F32) * (nn(gm, values[...]) - dot_sum)).astype(BF)
        S.pair_s[h][...] = ds
        y = nn(ds, jnp.where(own, k2, none))
        dq = y if dq is None else dq + y
    S.proj[:, at128(p)] = (dq * 0.125).astype(BF)
    dk = tn(S.pair_q[0][...], S.pair_s[0][...]) + tn(S.pair_q[1][...], S.pair_s[1][...])
    dv = tn(S.pair_g[0][...], S.probs(2 * p)[...]) + tn(S.pair_g[1][...], S.probs(2 * p + 1)[...])
    S.proj[:, at128(n + p)] = (dk.T * 0.125).astype(BF)
    S.proj[:, at128(2 * n + p)] = dv.T.astype(BF)


def first_back(S):
    n = S.t // 2
    for k in (6, 7, 10, 11):
        S.small[k : k + 1, :] = jnp.zeros((1, S.d), F32)

    def f(i):
        at = pl.ds(pl.multiple_of(i * n, 32), n)
        gf = None
        for c in range(3):
            y = nn(S.proj[at, c * S.d : (c + 1) * S.d], part_matrix(S, S.own, c))
            gf = y if gf is None else gf + y
        u, inv = standardize(S.x[at, :].astype(F32))
        S.grad[at, :] = (S.middle[at, :] + norm_back(gf, u, inv, S.vec[GAIN_ONE : GAIN_ONE + 1, :])).astype(BF)
        S.small[6:7, :] += jnp.sum(gf * u, 0, keepdims=True)
        S.small[7:8, :] += jnp.sum(gf, 0, keepdims=True)
        S.small[10:11, :] += jnp.sum(S.proj[at, 0 : S.d].astype(F32), 0, keepdims=True)
        S.small[11:12, :] += jnp.sum(S.proj[at, 2 * S.d : 3 * S.d].astype(F32), 0, keepdims=True)

    loop(2, f)


def inproj_grad(S):
    for c in range(3):
        store_part(S, c, tn(S.proj[:, c * S.d : (c + 1) * S.d], S.normed[...]).astype(BF))


class Links:
    def __init__(self, n_dp):
        self.dp = lax.axis_index("dp")
        self.t = lax.axis_index("tensor")
        self.c = self.dp % 2
        bx = (self.dp // 2) % 2
        by = (self.dp // 4) % 2
        self.b1 = bx + self.c * (by - bx)
        self.b2 = by + self.c * (bx - by)
        self.sib = self.dp + 1 - 2 * self.c
        self.p1 = self.dp + (1 - 2 * self.b1) * (2 + 2 * self.c)
        self.p2 = self.dp + (1 - 2 * self.b2) * (4 - 2 * self.c)
        self.more = []
        step = 8
        while step < n_dp:
            self.more.append(self.dp + (1 - 2 * ((self.dp // step) % 2)) * step)
            step *= 2

    def peer(self, r):
        return (self.t + r) % NZ

    def to(self, dp=None, t=None):
        return {"dp": self.dp if dp is None else dp, "tensor": self.t if t is None else t}


def remote(src, dst, ssem, rsem, to):
    return pltpu.make_async_remote_copy(
        src_ref=src, dst_ref=dst, send_sem=ssem, recv_sem=rsem, device_id=to, device_id_type=MESH
    )


class Gather:
    def __init__(self, S, L, k, chunk, base, n):
        d = S.d
        ch = k
        q, h = n // 4, d // 2
        cols = pl.ds(pl.multiple_of(L.c * h, 128), h)
        w = S.w[chunk]

        def quarter(k):
            return pl.ds(base + pl.multiple_of(k * q, 16), q)

        mine = quarter(2 * L.b2 + L.b1)
        near = quarter(2 * L.b2 + 1 - L.b1)
        upper = pl.ds(base + pl.multiple_of(L.b2 * 2 * q, 16), 2 * q)
        lower = pl.ds(base + pl.multiple_of((1 - L.b2) * 2 * q, 16), 2 * q)
        ss, rs = S.gsend, S.grecv
        src = w.at[0]
        self.z = [
            remote(src.at[mine, cols], w.at[r, mine, cols], ss.at[ch, r - 1], rs.at[ch, r - 1], L.to(t=L.peer(NZ - r)))
            for r in range(1, NZ)
        ]
        far = pl.ds(1, NZ - 1)
        self.one = remote(w.at[far, mine, cols], w.at[far, mine, cols], ss.at[ch, 3], rs.at[ch, 3], L.to(dp=L.p1))
        self.two = remote(w.at[far, upper, cols], w.at[far, upper, cols], ss.at[ch, 4], rs.at[ch, 4], L.to(dp=L.p2))
        self.sib = [
            remote(w.at[far, k, cols], w.at[far, k, cols], ss.at[ch, 5 + i], rs.at[ch, 5 + i], L.to(dp=L.sib))
            for i, k in enumerate((mine, near, lower))
        ]

    def start(self):
        for k in self.z:
            k.start()

    def after_z(self):
        for k in self.z:
            k.wait_recv()
        self.one.start()
        self.sib[0].start()

    def after_one(self):
        self.one.wait_recv()
        self.two.start()
        self.sib[1].start()

    def after_two(self):
        self.two.wait_recv()
        self.sib[2].start()

    def finish(self):
        for k in self.sib:
            k.wait_recv()

    def drain(self):
        for k in self.z + [self.one, self.two] + self.sib:
            k.wait_send()


class Reduce:
    def __init__(self, S, L, ch):
        d = S.d
        q, h = d // 4, d // 2
        self.S, self.L, self.ch, self.q, self.h = S, L, ch, q, h
        w = S.con_grad if ch == CON else S.w[ch]
        self.w = w
        self.c0 = pl.multiple_of(L.c * h, 128)
        cols = pl.ds(self.c0, h)
        other = pl.ds(pl.multiple_of((1 - L.c) * h, 128), h)
        self.cols = cols

        def quarter(k):
            return pl.ds(pl.multiple_of(k * q, 64), q)

        self.q0 = pl.multiple_of((2 * L.b2 + L.b1) * q, 64)
        mine = pl.ds(self.q0, q)
        near = quarter(2 * L.b2 + 1 - L.b1)
        self.u0 = pl.multiple_of(L.b2 * h, 128)
        upper = pl.ds(self.u0, h)
        lower = pl.ds(pl.multiple_of((1 - L.b2) * h, 128), h)
        ss, rs = S.rsend, S.rrecv
        out = S.gout.at[ch]
        self.core = remote(w.at[:, :, other], S.r1.at[ch], ss.at[ch, 0], rs.at[ch, 0], L.to(dp=L.sib))
        late = {EXP: 0, ATT: 1}.get(ch)
        self.r2 = S.r2 if late is None else S.r1.at[CON, :, late * h : late * h + h]
        self.r3 = S.r3 if late is None else S.r2.at[:, late * q : late * q + q]
        self.two = remote(w.at[:, lower, cols], self.r2, ss.at[ch, 1], rs.at[ch, 1], L.to(dp=L.p2))
        self.one = remote(w.at[:, near, cols], self.r3, ss.at[ch, 2], rs.at[ch, 2], L.to(dp=L.p1))
        self.z = [
            remote(w.at[r, mine, cols], S.r4.at[ch, NZ - 1 - r], ss.at[ch, 2 + r], rs.at[ch, 6 - r], L.to(t=L.peer(r)))
            for r in range(1, NZ)
        ]
        self.more = [
            remote(S.r4.at[ch, i], S.r5.at[ch, i], ss.at[ch, 11 + i], rs.at[ch, 11 + i], L.to(dp=m))
            for i, m in enumerate(L.more)
        ]
        own = w.at[0, mine, cols]
        self.keep = pltpu.make_async_copy(own, out.at[mine, cols], S.lsem.at[3 + ch])
        self.back_one = remote(own, out.at[mine, cols], ss.at[ch, 6], rs.at[ch, 6], L.to(dp=L.p1))
        self.back_two = remote(out.at[upper, cols], out.at[upper, cols], ss.at[ch, 7], rs.at[ch, 7], L.to(dp=L.p2))
        self.back_sib = [
            remote(own, out.at[mine, cols], ss.at[ch, 8], rs.at[ch, 8], L.to(dp=L.sib)),
            remote(out.at[near, cols], out.at[near, cols], ss.at[ch, 9], rs.at[ch, 9], L.to(dp=L.sib)),
            remote(out.at[lower, cols], out.at[lower, cols], ss.at[ch, 10], rs.at[ch, 10], L.to(dp=L.sib)),
        ]

    def start(self):
        self.core.start()

    def add(self, src, first, count):
        w, cols = self.w, self.cols
        step = self.q

        def f(i):
            r, k = i // (count // step), i % (count // step)
            at = pl.ds(first + pl.multiple_of(k * step, 64), step)
            got = src[r, pl.ds(pl.multiple_of(k * step, 64), step), :].astype(F32)
            w[r, at, cols] = (w[r, at, cols].astype(F32) + got).astype(BF)

        loop(NZ * (count // step), f)

    def merge_core(self):
        self.core.wait()
        self.add(self.S.r1.at[self.ch], 0, 2 * self.h)

    def after_core(self):
        self.merge_core()
        self.two.start()

    def after_two(self):
        self.two.wait()
        self.add(self.r2, self.u0, self.h)
        self.one.start()

    def after_one(self):
        self.one.wait()
        self.add(self.r3, self.q0, self.q)
        for k in self.z:
            k.start()

    def after_z(self):
        S, w = self.S, self.w
        for k in self.z:
            k.wait()
        mine = pl.ds(self.q0, self.q)
        v = w[0, mine, self.cols].astype(F32)
        for k in range(NZ - 1):
            v = v + S.r4[self.ch, k].astype(F32)
        for i, k in enumerate(self.more):
            S.r4[self.ch, i] = v.astype(BF)
            k.start()
            k.wait()
            v = S.r4[self.ch, i].astype(F32) + S.r5[self.ch, i].astype(F32)
        w[0, mine, self.cols] = v.astype(BF)
        self.keep.start()
        self.back_one.start()
        self.back_sib[0].start()

    def after_back_one(self):
        self.keep.wait()
        self.back_one.wait()
        self.back_two.start()
        self.back_sib[1].start()

    def after_back_two(self):
        self.back_two.wait()
        self.back_sib[2].start()

    def finish(self):
        for k in self.back_sib:
            k.wait()


class Spread:
    def __init__(self, S, L, own, out):
        self.t = L.t
        right, left = L.to(t=(L.t + 1) % NZ), L.to(t=(L.t + NZ - 1) % NZ)
        ss, rs = S.osend, S.orecv

        def block(j):
            return out.at[(L.t + j + NZ) % NZ]

        self.keep = pltpu.make_async_copy(own, out.at[L.t], S.lsem.at[6])
        self.side = [
            [remote(own if i == 0 else block(-i), block(-i), ss.at[i], rs.at[i], right) for i in range(NZ - 1)],
            [remote(own if i == 0 else block(i), block(i), ss.at[3 + i], rs.at[3 + i], left) for i in range(NZ - 1)],
        ]

    def when_sent(self, i, f):
        pl.when((self.t >= i) & (self.t < NZ - 1))(lambda: f(self.side[0][i]))
        pl.when((self.t <= NZ - 1 - i) & (self.t > 0))(lambda: f(self.side[1][i]))

    def start(self):
        self.keep.start()
        self.send(0)

    def send(self, i):
        self.when_sent(i, lambda k: k.start())

    def arrive(self, i):
        pl.when(self.t >= i + 1)(lambda: self.side[0][i].wait_recv())
        pl.when(self.t <= NZ - 2 - i)(lambda: self.side[1][i].wait_recv())

    def forward(self, i):
        self.arrive(i - 1)
        self.send(i)

    def finish(self):
        self.keep.wait()
        self.arrive(NZ - 2)
        for i in range(NZ - 1):
            self.when_sent(i, lambda k: k.wait_send())


class SmallSum:
    def __init__(self, S, L):
        self.S = S
        ss, rs = S.ssend, S.srecv
        partners = [L.sib, L.p1, L.p2] + L.more
        self.rounds = [
            remote(S.small_out.at[i], S.small_in.at[i], ss.at[i], rs.at[i], L.to(dp=p)) for i, p in enumerate(partners)
        ]
        n = len(partners)
        self.L = L
        self.z = [
            remote(S.small, S.sums.at[L.t], ss.at[n + r - 1], rs.at[n + NZ - 1 - r], L.to(t=L.peer(r)))
            for r in range(1, NZ)
        ]

    def start(self, i):
        self.S.small_out[i] = self.S.small[...]
        self.rounds[i].start()

    def after(self, i):
        self.rounds[i].wait()
        self.S.small[...] += self.S.small_in[i]
        if i + 1 < len(self.rounds):
            self.start(i + 1)
        else:
            for k in self.z:
                k.start()

    def finish(self):
        S, t = self.S, self.L.t
        for k in self.z:
            k.wait()
        S.sums[t] = S.small[...]
        total = S.sums[0] + S.sums[1] + S.sums[2] + S.sums[3]
        S.vec_out[...] = total
        w = S.d // NZ
        hidden = jnp.zeros((1, S.d), F32)
        heads = jnp.zeros((8, S.d), F32)
        for k in range(NZ):
            r = (t + NZ - k) % NZ
            hidden = hidden + S.sums[k, pl.ds(r, 1), :]
            heads = heads + pltpu.roll(S.sums[k, 8:16, :], ((NZ - r) % NZ) * w, 1)
        S.vec_out[0:1, :] = hidden
        S.vec_out[1:3, :] = heads[2:4, :]


NAMES_IN = ("tokens", "cot", "segments", "wi", "wo", "we", "wc", "qb", "vb", "eb", "ob", "g1", "s1", "g2", "s2", "cb")
NAMES_OUT = ("layers", "token_grads", "gout", "vec_out", "kept")


def layer_kernel(n_dp, names, *refs):
    S = Bag()
    for n, r in zip(names, refs):
        setattr(S, n, r)
    S.t, S.d = S.x.shape
    t, d = S.t, S.d
    n_heads, pairs = d // 64, d // 128
    S.w = [S.wbuf.at[0], S.wbuf.at[1], S.wbuf.at[2]]
    S.vec = S.table.at[pl.ds(8, 8)]
    L = Links(n_dp)

    def pool(first, n):
        return S.pool.at[pl.ds(pl.multiple_of(first, 64), n)]

    S.probs = lambda i: S.pool.at[pl.ds(pl.multiple_of(i * t, 64), t), 0:t]
    S.slope = lambda r: pool((n_heads + NZ + r) * t, t)
    spare = [S.pool.at[(n_heads + NZ + r) * t : (n_heads + NZ + r + 1) * t] for r in range(NZ)]
    S.seg_q = [spare[2].at[:, 128 * h : 128 * h + 128] for h in (0, 1)]
    S.seg_k = [spare[2].at[:, 256 + 128 * h : 384 + 128 * h] for h in (0, 1)]
    S.keys_t = [spare[3].at[128 * h : 128 * h + 128, 0:t] for h in (0, 1)]
    S.pair_s = [S.wbuf.at[EXP, h, 0:t, 0:t] for h in (0, 1)]
    S.pair_g = [S.wbuf.at[EXP, 2, 0:t, 128 * h : 128 * h + 128] for h in (0, 1)]
    S.pair_q = [S.wbuf.at[EXP, 2, 0:t, 256 + 128 * h : 384 + 128 * h] for h in (0, 1)]
    S.values_t = S.wbuf.at[EXP, 3, 0:128, 0:t]
    S.grad = S.up

    own, other = Bag(), Bag()
    own.x, own.normed, own.proj, own.heads, own.middle = S.x, S.normed, S.proj, S.heads, S.middle
    own.second, own.keep, own.active = S.second, True, lambda r: pool((n_heads + r) * t, t)
    own.weight = lambda ch, r: S.wbuf.at[ch, r]
    other.x, other.normed, other.proj, other.heads, other.middle = S.x, S.heads, S.proj, S.gheads, S.middle
    other.second, other.keep, other.active = S.branch, False, S.slope
    other.weight = lambda ch, r: S.wbuf.at[ch, r] if ch == CON else pool((ch * NZ + r) * d, d)
    S.own = own

    barrier = pltpu.get_barrier_semaphore()
    partners = [L.to(dp=p) for p in [L.sib, L.p1, L.p2] + L.more] + [L.to(t=L.peer(r)) for r in range(1, NZ)]
    for p in partners:
        pl.semaphore_signal(barrier, inc=1, device_id=p, device_id_type=MESH)
    w = d // NZ
    shards = [
        pltpu.make_async_copy(S.wi, S.w[ATT].at[0, 0 : 3 * w], S.lsem.at[0]),
        pltpu.make_async_copy(S.wo, S.w[ATT].at[0, 3 * w : 4 * w], S.lsem.at[1]),
        pltpu.make_async_copy(S.we, S.w[EXP].at[0], S.lsem.at[2]),
        pltpu.make_async_copy(S.wc, S.w[CON].at[0], S.lsem.at[7]),
    ]
    load_x = pltpu.make_async_copy(S.tokens.at[L.t], S.x, S.lsem.at[8])
    load_up = pltpu.make_async_copy(S.cot.at[L.t], S.up, S.lsem.at[9])
    for k in shards + [load_x, load_up]:
        k.start()
    save = [[pltpu.make_async_copy(S.wbuf.at[c, r], S.kept.at[c, r], S.saved.at[c, r]) for r in range(NZ)] for c in range(2)]
    reload = [
        [pltpu.make_async_copy(S.kept.at[c, r], other.weight(c, r), S.loaded.at[c, r]) for r in range(NZ)] for c in range(2)
    ]

    def every(copies, what):
        for k in copies:
            getattr(k, what)()

    bias = [
        remote(S.table.at[pl.ds(0, 8)], S.bias.at[r], S.bsend.at[r - 1], S.brecv.at[r - 1], L.to(t=L.peer(NZ - r)))
        for r in range(1, NZ)
    ]
    third = d // 3
    parts = [(ATT, w * i, w) for i in range(NZ)] + [(ch, third * i, third) for ch in (EXP, CON) for i in range(3)]
    G = [Gather(S, L, k, *part) for k, part in enumerate(parts)]
    R = [Reduce(S, L, ch) for ch in range(3)]
    tokens = Spread(S, L, S.grad, S.token_grads)
    small = SmallSum(S, L)
    put_own = pltpu.make_async_copy(S.layer, S.layers.at[L.t], S.lsem.at[10])

    def gather(k):
        n = len(G)
        if k < n:
            G[k].after_z()
            if k + 2 < n:
                G[k + 2].start()
        if 0 <= k - 1 < n:
            G[k - 1].after_one()
        if 0 <= k - 2 < n:
            G[k - 2].after_two()

    def load_other(i):
        return pltpu.make_async_copy(S.tokens.at[L.peer(i + 1)], S.x, S.lsem.at[11])

    def put_other(i):
        return pltpu.make_async_copy(S.layer, S.layers.at[L.peer(i + 1)], S.lsem.at[12])

    S.table[...] = jnp.zeros_like(S.table)
    for row, ref in ((0, S.qb), (2, S.vb), (3, S.eb)):
        S.table[row : row + 1, 0 : ref.shape[0]] = ref[...].astype(F32).reshape(1, ref.shape[0])
    for row, ref in enumerate((S.ob, S.g1, S.s1, S.g2, S.s2, S.cb)):
        S.table[8 + row : 9 + row, :] = ref[...].astype(F32).reshape(1, d)
    S.bias[0] = S.table[0:8, :]
    every(shards[:2], "wait")
    pl.semaphore_wait(barrier, len(partners))
    G[0].start()
    G[1].start()
    every(bias, "start")
    every(shards[2:], "wait")
    segment_tables(S, L.t)
    load_x.wait()
    first_norm(S, own)
    gather(0)
    every(bias, "wait")
    set_bias(S)
    gather(1)
    for c in range(3):
        gather(c + 2)
        G[c].finish()
        project(S, own, c)

    def pair(p):
        attend_pair(S, own, p)
        pl.when(p == 1)(lambda: gather(5))
        pl.when(p == 4)(lambda: gather(6))

    loop(pairs, pair)
    G[3].finish()
    every(save[ATT], "start")
    attend_out(S, own)
    load_up.wait()
    mask_upstream(S)
    gather(7)
    gather(8)
    for k in (4, 5, 6):
        G[k].finish()
    every(save[EXP], "start")
    expand_up(S, own, lambda r: pl.when(r == 2)(lambda: gather(9)))
    contract_grad(S, lambda r: pl.when(r == 2)(lambda: gather(10)))
    R[CON].start()
    G[7].finish()
    hidden_back(S, 0, third)
    G[8].finish()
    hidden_back(S, 1, third)
    R[CON].merge_core()
    gather(11)
    R[CON].two.start()
    G[9].finish()
    hidden_back(S, 2, third)

    S.layer[...] = S.middle[...].astype(BF)
    second_back(S)
    heads_back(S)
    for g in G:
        g.drain()
    for c in range(2):
        every(save[c], "wait")

    def pair_back(p):
        attend_back_pair(S, p)
        pl.when(p == 4)(R[CON].after_two)

    loop(pairs, pair_back)
    first_back(S)
    tokens.start()
    small.start(0)
    load_other(0).start()
    for c in range(2):
        every(reload[c], "start")
    expand_grad(S)
    R[EXP].start()
    R[CON].after_one()
    outproj_grad(S)
    inproj_grad(S)
    R[EXP].after_core()
    R[ATT].start()
    contract_down(S, own)
    put_own.start()

    def rounds():
        for i in range(2, 3 + len(L.more)):
            small.after(i)

    steps = {
        (0, 0): [lambda: small.after(0), R[ATT].after_core],
        (0, 3): [lambda: small.after(1)],
        (0, 6): [rounds],
        (0, 7): [lambda: tokens.forward(1)],
        (0, 9): [R[CON].after_z],
        (1, 0): [R[EXP].after_two],
        (1, 1): [R[CON].after_back_one],
        (1, 2): [R[ATT].after_two],
        (1, 4): [R[CON].after_back_two],
        (1, 5): [R[EXP].after_one],
        (1, 8): [R[ATT].after_one, lambda: tokens.forward(2)],
        (2, 2): [R[EXP].after_z],
        (2, 4): [R[EXP].after_back_one],
        (2, 6): [R[ATT].after_z, R[EXP].after_back_two],
        (2, 7): [small.finish],
        (2, 8): [R[ATT].after_back_one],
        (2, 9): [R[ATT].after_back_two],
    }

    def at(i, q):
        for (si, sq), fs in steps.items():
            if isinstance(q, int):
                if sq == q:
                    pl.when(i == si)(lambda fs=fs: [f() for f in fs] and None)
            elif 1 <= sq <= pairs:
                pl.when((i == si) & (q == sq))(lambda fs=fs: [f() for f in fs] and None)

    def forward_other(i):
        load_other(i).wait()
        pl.when(i == 0)(lambda: every(reload[ATT], "wait"))
        segment_tables(S, L.peer(i + 1))
        first_norm(S, other)
        for c in range(3):
            project(S, other, c)
        at(i, 0)

        def pair_other(p):
            attend_pair(S, other, p)
            at(i, p + 1)

        loop(pairs, pair_other)
        attend_out(S, other)
        pl.when(i < NZ - 2)(lambda: load_other(i + 1).start())
        at(i, 7)
        pl.when(i == 0)(lambda: every(reload[EXP], "wait"))
        expand_up(S, other)
        at(i, 8)
        pl.when(i > 0)(lambda: put_other(i - 1).wait())
        pl.when(i == 0)(put_own.wait)
        contract_down(S, other)
        put_other(i).start()
        at(i, 9)

    loop(NZ - 1, forward_other)
    put_other(NZ - 2).wait()
    for r in R:
        r.finish()
    tokens.finish()


def run_layer(n_dp, tokens, cot, segments, wi, wo, we, wc, *vectors):
    _, t, d = tokens.shape
    more = max(n_dp.bit_length() - 1 - 3, 0)
    spare = max(more, 1)
    any_, vmem = pl.BlockSpec(memory_space=pl.ANY), pl.BlockSpec(memory_space=pltpu.VMEM)
    V, DMA = pltpu.VMEM, pltpu.SemaphoreType.DMA
    scratch = dict(
        x=V((t, d), BF),
        up=V((t, d), BF),
        normed=V((t, d), BF),
        proj=V((t, 3 * d), BF),
        heads=V((t, d), BF),
        pool=V(((d // 64 + 2 * NZ) * t, d), BF),
        middle=V((t, d), F32),
        second=V((t, d), BF),
        branch=V((t, d), BF),
        gheads=V((t, d), BF),
        seg_col=V((t, 128), F32),
        sums=V((NZ, 16, d), F32),
        layer=V((t, d), BF),
        inv_sum=V((t, 128), F32),
        wbuf=V((3, NZ, d, d), BF),
        con_grad=V((NZ, d, d), BF),
        table=V((16, d), F32),
        bias=V((NZ, 8, d), F32),
        qkv_bias=V((8, d), F32),
        small=V((16, d), F32),
        small_in=V((3 + more, 16, d), F32),
        small_out=V((3 + more, 16, d), F32),
        r1=V((3, NZ, d, d // 2), BF),
        r2=V((NZ, d // 2, d // 2), BF),
        r3=V((NZ, d // 4, d // 2), BF),
        r4=V((3, NZ - 1, d // 4, d // 2), BF),
        r5=V((3, spare, d // 4 if more else 16, d // 2), BF),
        lsem=DMA((13,)),
        gsend=DMA((10, 8)),
        grecv=DMA((10, 8)),
        rsend=DMA((3, 11 + spare)),
        rrecv=DMA((3, 11 + spare)),
        osend=DMA((6,)),
        orecv=DMA((6,)),
        saved=DMA((2, NZ)),
        loaded=DMA((2, NZ)),
        ssend=DMA((6 + more,)),
        srecv=DMA((6 + more,)),
        bsend=DMA((3,)),
        brecv=DMA((3,)),
    )
    names = NAMES_IN + NAMES_OUT + tuple(scratch)
    out_shape = [
        jax.ShapeDtypeStruct((NZ, t, d), BF),
        jax.ShapeDtypeStruct((NZ, t, d), BF),
        jax.ShapeDtypeStruct((3, d, d), BF),
        jax.ShapeDtypeStruct((16, d), F32),
        jax.ShapeDtypeStruct((2, NZ, d, d), BF),
    ]
    return pl.pallas_call(
        functools.partial(layer_kernel, n_dp, names),
        out_shape=out_shape,
        in_specs=[any_, any_, vmem, any_, any_, any_, any_] + [vmem] * len(vectors),
        out_specs=[any_] * 3 + [vmem, any_],
        scratch_shapes=list(scratch.values()),
        compiler_params=pltpu.CompilerParams(
            collective_id=0, has_side_effects=True, vmem_limit_bytes=63 << 20
        ),
        name="layer",
    )(tokens, cot, segments, wi, wo, we, wc, *vectors)


def local(
    n_dp,
    tokens,
    segments,
    cotangent,
    inproj,
    querybias,
    valuebias,
    outproj,
    outbias,
    gainone,
    shiftone,
    gaintwo,
    shifttwo,
    expand,
    expandbias,
    contract,
    contractbias,
):
    _, t, d = tokens.shape
    w = d // NZ
    wi = inproj.transpose(1, 2, 0).reshape(3 * w, d)
    vectors = (querybias, valuebias, expandbias, outbias, gainone, shiftone, gaintwo, shifttwo, contractbias)
    layers, token_grads, gout, vec, _ = run_layer(n_dp, tokens, cotangent, segments, wi, outproj, expand, contract, *vectors)
    ga = gout[ATT].astype(F32)
    return (
        layers,
        token_grads,
        ga[: 3 * w].reshape(3, w, d).transpose(2, 0, 1),
        vec[1, :w],
        vec[2, :w],
        ga[3 * w :],
        vec[5],
        vec[6],
        vec[7],
        vec[8],
        vec[9],
        gout[EXP].astype(F32),
        vec[0],
        gout[CON].astype(F32),
        vec[4],
    )


def solution(mesh):
    in_specs = (
        P("dp", None, None),
        P("dp", None),
        P("dp", None, None),
        P(None, None, "tensor"),
        P("tensor"),
        P("tensor"),
        P("tensor", None),
        P(),
        P(),
        P(),
        P(),
        P(),
        P(None, "tensor"),
        P("tensor"),
        P("tensor", None),
        P(),
    )
    out_specs = (
        P("dp", None, None),
        P("dp", None, None),
        P(None, None, "tensor"),
        P("tensor"),
        P("tensor"),
        P("tensor", None),
        P(),
        P(),
        P(),
        P(),
        P(),
        P(None, "tensor"),
        P("tensor"),
        P("tensor", None),
        P(),
    )
    return jax.shard_map(
        functools.partial(local, mesh.shape["dp"]),
        mesh=mesh,
        in_specs=in_specs,
        out_specs=out_specs,
        check_vma=False,
    )
```

```python
import functools

import jax
import jax.numpy as jnp
from jax import lax
from jax.experimental import pallas as pl
from jax.experimental.pallas import tpu as pltpu
from jax.sharding import PartitionSpec as P

BF = jnp.bfloat16
F32 = jnp.float32
EPSILON = 1e-06
LOG2E = 1.4426950408889634
ROOT_HALF = 0.7071067811865476
INV_ROOT_TWO_PI = 0.3989422804014327
MESH = pl.DeviceIdType.MESH
RT = 192
APART = 2.0**100
NZ = 4
OUT_BIAS, GAIN_ONE, SHIFT_ONE, GAIN_TWO, SHIFT_TWO, CONTRACT_BIAS = range(6)
ATT, EXP, CON = range(3)


def nt(a, b):
    return lax.dot_general(a, b, (((1,), (1,)), ((), ())), preferred_element_type=F32)


def nn(a, b):
    return lax.dot_general(a, b, (((1,), (0,)), ((), ())), preferred_element_type=F32)


def tn(a, b):
    return lax.dot_general(a, b, (((0,), (0,)), ((), ())), preferred_element_type=F32)


def at128(i):
    return pl.ds(pl.multiple_of(i * 128, 128), 128)


def at256(i):
    return pl.ds(pl.multiple_of(i * 256, 256), 256)


def rows(i):
    return pl.ds(pl.multiple_of(i * RT, RT), RT)


def loop(n, f):
    def body(i, carry):
        f(i)
        return carry

    lax.fori_loop(0, n, body, 0)


def standardize(v):
    mu = jnp.mean(v, -1, keepdims=True)
    c = v - mu
    inv = lax.rsqrt(jnp.mean(c * c, -1, keepdims=True) + EPSILON)
    return c * inv, inv


def norm_back(z, unit, inv, gain):
    s = z * gain
    a = jnp.mean(s, -1, keepdims=True)
    b = jnp.mean(s * unit, -1, keepdims=True)
    return inv * (s - a - unit * b)


def head_lanes(shape, h):
    lane = lax.broadcasted_iota(jnp.int32, shape, 1)
    return (lane < 64) if h == 0 else (lane >= 64)


class Bag:
    pass


def segment_column(S, t):
    row = S.segments[pl.ds(t, 1), :].astype(F32)
    S.seg_col[...] = jnp.broadcast_to(row, (128, S.t)).T


def segment_tables(S, t):
    segment_column(S, t)
    lane = lax.broadcasted_iota(jnp.int32, (S.t, 128), 1)
    ids = S.seg_col[...].astype(jnp.int32)
    for h in (0, 1):
        at = lane - (64 if h == 0 else 0)
        same = at == ids
        S.seg_q[h][...] = jnp.where(same, 1.0, 0.0).astype(BF)
        S.seg_k[h][...] = jnp.where((at >= 0) & (at < 8) & (~same), -APART, 0.0).astype(BF)


def first_norm(S, B):
    u, _ = standardize(B.x[...].astype(F32))
    B.normed[...] = (
        u * S.vec[GAIN_ONE : GAIN_ONE + 1, :] + S.vec[SHIFT_ONE : SHIFT_ONE + 1, :]
    ).astype(BF)


def set_bias(S):
    placed = S.bias[0]
    for r in range(1, NZ):
        placed = placed + pltpu.roll(S.bias[r], r * (S.d // NZ), 1)
    S.qkv_bias[...] = placed


def part_matrix(S, B, c):
    w = S.d // NZ
    return jnp.concatenate([B.weight(ATT, r)[c * w : (c + 1) * w, :] for r in range(NZ)], 0)


def project(S, B, c):
    y = nt(B.normed[...], part_matrix(S, B, c)) + S.qkv_bias[c : c + 1, :]
    B.proj[:, c * S.d : (c + 1) * S.d] = y.astype(BF)


def attend_pair(S, B, p):
    n = S.d // 128
    k2 = B.proj[:, at128(n + p)]
    v2 = B.proj[:, at128(2 * n + p)]
    q2 = B.proj[:, at128(p)]
    lane = lax.broadcasted_iota(jnp.int32, (S.t, 128), 1)
    outs, sums = [], []
    for h in (0, 1):
        own = head_lanes(q2.shape, h)
        one = lane == (64 if h == 0 else 0)
        flat = S.keys_t[h]
        flat[...] = jnp.where(own, k2, S.seg_k[h][...]).T
        s = nn(jnp.where(own, q2, S.seg_q[h][...]), flat[...])
        e = jnp.exp2((s - jnp.max(s, -1, keepdims=True)) * (0.125 * LOG2E)).astype(BF)
        if B.keep:
            S.probs(2 * p + h)[...] = e
        o = nn(e, jnp.where(own, v2, jnp.where(one, 1.0, 0.0).astype(BF)))
        at = 64 if h == 0 else 0
        sums.append(1.0 / o[:, at : at + 1])
        outs.append(o)
    first = head_lanes(outs[0].shape, 0)
    scale = jnp.where(first, sums[0], sums[1])
    if B.keep:
        kept = jnp.where(lane == 2 * p, sums[0], S.inv_sum[...])
        S.inv_sum[...] = jnp.where(lane == 2 * p + 1, sums[1], kept)
    B.heads[:, at128(p)] = (jnp.where(first, outs[0], outs[1]) * scale).astype(BF)


def attend_out(S, B):
    m = B.x[...].astype(F32) + nn(B.heads[...], part_matrix(S, B, 3)) + S.vec[OUT_BIAS : OUT_BIAS + 1, :]
    B.middle[...] = m
    u, _ = standardize(m)
    B.second[...] = (
        u * S.vec[GAIN_TWO : GAIN_TWO + 1, :] + S.vec[SHIFT_TWO : SHIFT_TWO + 1, :]
    ).astype(BF)


def expand_up(S, B, done=lambda r: None):
    def g(r):
        w = B.weight(EXP, r)
        for j in range(S.d // 256):
            c = slice(256 * j, 256 * j + 256)
            h = nn(B.second[...], w[:, c]) + S.bias[r, 3:4, c]
            cdf = 0.5 + 0.5 * lax.erf(h * ROOT_HALF)
            B.active(r)[:, c] = (h * cdf).astype(BF)
            if B.keep:
                S.slope(r)[:, c] = (cdf + h * jnp.exp2(h * h * (-0.5 * LOG2E)) * INV_ROOT_TWO_PI).astype(BF)
        done(r)

    loop(NZ, g)


def contract_down(S, B):
    a = (S.layer if B.keep else B.middle)[...].astype(F32) + S.vec[CONTRACT_BIAS : CONTRACT_BIAS + 1, :]
    for r in range(NZ):
        a = a + nn(B.active(r)[...], B.weight(CON, r)[...])
    S.layer[...] = a.astype(BF)


def mask_upstream(S):
    S.small[...] = jnp.zeros_like(S.small)
    g = jnp.where(S.seg_col[:, 0:1] > 0.0, S.up[...].astype(F32), 0.0)
    S.up[...] = g.astype(BF)
    S.small[4:5, :] = jnp.sum(g, 0, keepdims=True)


def hidden_back(S, j, n):
    c = slice(n * j, n * j + n)

    def f(r):
        gh = (nt(S.up[...], S.wbuf[CON, r, c, :]) * S.slope(r)[:, c].astype(F32)).astype(BF)
        S.slope(r)[:, c] = gh
        S.small[pl.ds(r, 1), c] = jnp.sum(gh.astype(F32), 0, keepdims=True)

    loop(NZ, f)


def contract_grad(S, done):
    def f(r):
        S.con_grad[r] = tn(S.own.active(r)[...], S.up[...]).astype(BF)
        done(r)

    loop(NZ, f)


def second_back(S):
    n = S.t // 2
    for k in (8, 9, 5):
        S.small[k : k + 1, :] = jnp.zeros((1, S.d), F32)

    def f(i):
        at = pl.ds(pl.multiple_of(i * n, 32), n)
        gs = nt(S.slope(0)[at, :], S.w[EXP][0])
        for r in range(1, NZ):
            gs = gs + nt(S.slope(r)[at, :], S.w[EXP][r])
        u, inv = standardize(S.middle[at, :])
        gm = S.up[at, :].astype(F32) + norm_back(gs, u, inv, S.vec[GAIN_TWO : GAIN_TWO + 1, :])
        S.middle[at, :] = gm
        gb = gm.astype(BF)
        S.branch[at, :] = gb
        S.small[8:9, :] += jnp.sum(gs * u, 0, keepdims=True)
        S.small[9:10, :] += jnp.sum(gs, 0, keepdims=True)
        S.small[5:6, :] += jnp.sum(gb.astype(F32), 0, keepdims=True)

    loop(2, f)


def expand_grad(S):
    def f(r):
        S.w[EXP][r] = tn(S.second[...], S.slope(r)[...]).astype(BF)

    loop(NZ, f)


def heads_back(S):
    S.gheads[...] = nt(S.branch[...], part_matrix(S, S.own, 3)).astype(BF)


def store_part(S, c, v):
    w = S.d // NZ
    for r in range(NZ):
        S.w[ATT][r, c * w : (c + 1) * w, :] = v[r * w : (r + 1) * w, :]


def outproj_grad(S):
    store_part(S, 3, tn(S.heads[...], S.branch[...]).astype(BF))


def attend_back_pair(S, p):
    n = S.d // 128
    q2 = S.proj[:, at128(p)]
    k2 = S.proj[:, at128(n + p)]
    v2 = S.proj[:, at128(2 * n + p)]
    lane = lax.broadcasted_iota(jnp.int32, (S.t, 128), 1)
    values = S.values_t
    values[...] = v2.T
    kept = S.inv_sum[...]
    scale = [jnp.sum(jnp.where(lane == 2 * p + h, kept, 0.0), -1, keepdims=True) for h in (0, 1)]
    first = head_lanes(q2.shape, 0)
    g2 = (S.gheads[:, at128(p)].astype(F32) * jnp.where(first, scale[0], scale[1])).astype(BF)
    od = g2.astype(F32) * S.heads[:, at128(p)].astype(F32)
    none = jnp.zeros_like(q2)
    dq = None
    for h in (0, 1):
        own = head_lanes(q2.shape, h)
        gm = jnp.where(own, g2, none)
        S.pair_g[h][...] = gm
        S.pair_q[h][...] = jnp.where(own, q2, none)
        dot_sum = jnp.sum(jnp.where(own, od, 0.0), -1, keepdims=True)
        ds = (S.probs(2 * p + h)[...].astype(F32) * (nn(gm, values[...]) - dot_sum)).astype(BF)
        S.pair_s[h][...] = ds
        y = nn(ds, jnp.where(own, k2, none))
        dq = y if dq is None else dq + y
    S.proj[:, at128(p)] = (dq * 0.125).astype(BF)
    dk = tn(S.pair_q[0][...], S.pair_s[0][...]) + tn(S.pair_q[1][...], S.pair_s[1][...])
    dv = tn(S.pair_g[0][...], S.probs(2 * p)[...]) + tn(S.pair_g[1][...], S.probs(2 * p + 1)[...])
    S.proj[:, at128(n + p)] = (dk.T * 0.125).astype(BF)
    S.proj[:, at128(2 * n + p)] = dv.T.astype(BF)


def first_back(S):
    n = S.t // 2
    for k in (6, 7, 10, 11):
        S.small[k : k + 1, :] = jnp.zeros((1, S.d), F32)

    def f(i):
        at = pl.ds(pl.multiple_of(i * n, 32), n)
        gf = None
        for c in range(3):
            y = nn(S.proj[at, c * S.d : (c + 1) * S.d], part_matrix(S, S.own, c))
            gf = y if gf is None else gf + y
        u, inv = standardize(S.x[at, :].astype(F32))
        S.grad[at, :] = (S.middle[at, :] + norm_back(gf, u, inv, S.vec[GAIN_ONE : GAIN_ONE + 1, :])).astype(BF)
        S.small[6:7, :] += jnp.sum(gf * u, 0, keepdims=True)
        S.small[7:8, :] += jnp.sum(gf, 0, keepdims=True)
        S.small[10:11, :] += jnp.sum(S.proj[at, 0 : S.d].astype(F32), 0, keepdims=True)
        S.small[11:12, :] += jnp.sum(S.proj[at, 2 * S.d : 3 * S.d].astype(F32), 0, keepdims=True)

    loop(2, f)


def inproj_grad(S):
    for c in range(3):
        store_part(S, c, tn(S.proj[:, c * S.d : (c + 1) * S.d], S.normed[...]).astype(BF))


class Links:
    def __init__(self, n_dp):
        self.dp = lax.axis_index("dp")
        self.t = lax.axis_index("tensor")
        self.c = self.dp % 2
        bx = (self.dp // 2) % 2
        by = (self.dp // 4) % 2
        self.b1 = bx + self.c * (by - bx)
        self.b2 = by + self.c * (bx - by)
        self.sib = self.dp + 1 - 2 * self.c
        self.p1 = self.dp + (1 - 2 * self.b1) * (2 + 2 * self.c)
        self.p2 = self.dp + (1 - 2 * self.b2) * (4 - 2 * self.c)
        self.more = []
        step = 8
        while step < n_dp:
            self.more.append(self.dp + (1 - 2 * ((self.dp // step) % 2)) * step)
            step *= 2

    def peer(self, r):
        return (self.t + r) % NZ

    def to(self, dp=None, t=None):
        return {"dp": self.dp if dp is None else dp, "tensor": self.t if t is None else t}


def remote(src, dst, ssem, rsem, to):
    return pltpu.make_async_remote_copy(
        src_ref=src, dst_ref=dst, send_sem=ssem, recv_sem=rsem, device_id=to, device_id_type=MESH
    )


class Gather:
    def __init__(self, S, L, k, chunk, base, n):
        d = S.d
        ch = k
        q, h = n // 4, d // 2
        cols = pl.ds(pl.multiple_of(L.c * h, 128), h)
        w = S.w[chunk]

        def quarter(k):
            return pl.ds(base + pl.multiple_of(k * q, 16), q)

        mine = quarter(2 * L.b2 + L.b1)
        near = quarter(2 * L.b2 + 1 - L.b1)
        upper = pl.ds(base + pl.multiple_of(L.b2 * 2 * q, 16), 2 * q)
        lower = pl.ds(base + pl.multiple_of((1 - L.b2) * 2 * q, 16), 2 * q)
        ss, rs = S.gsend, S.grecv
        src = w.at[0]
        self.z = [
            remote(src.at[mine, cols], w.at[r, mine, cols], ss.at[ch, r - 1], rs.at[ch, r - 1], L.to(t=L.peer(NZ - r)))
            for r in range(1, NZ)
        ]
        far = pl.ds(1, NZ - 1)
        self.one = remote(w.at[far, mine, cols], w.at[far, mine, cols], ss.at[ch, 3], rs.at[ch, 3], L.to(dp=L.p1))
        self.two = remote(w.at[far, upper, cols], w.at[far, upper, cols], ss.at[ch, 4], rs.at[ch, 4], L.to(dp=L.p2))
        self.sib = [
            remote(w.at[far, k, cols], w.at[far, k, cols], ss.at[ch, 5 + i], rs.at[ch, 5 + i], L.to(dp=L.sib))
            for i, k in enumerate((mine, near, lower))
        ]

    def start(self):
        for k in self.z:
            k.start()

    def after_z(self):
        for k in self.z:
            k.wait_recv()
        self.one.start()
        self.sib[0].start()

    def after_one(self):
        self.one.wait_recv()
        self.two.start()
        self.sib[1].start()

    def after_two(self):
        self.two.wait_recv()
        self.sib[2].start()

    def finish(self):
        for k in self.sib:
            k.wait_recv()

    def drain(self):
        for k in self.z + [self.one, self.two] + self.sib:
            k.wait_send()


class Reduce:
    def __init__(self, S, L, ch):
        d = S.d
        q, h = d // 4, d // 2
        self.S, self.L, self.ch, self.q, self.h = S, L, ch, q, h
        w = S.con_grad if ch == CON else S.w[ch]
        self.w = w
        self.c0 = pl.multiple_of(L.c * h, 128)
        cols = pl.ds(self.c0, h)
        other = pl.ds(pl.multiple_of((1 - L.c) * h, 128), h)
        self.cols = cols

        def quarter(k):
            return pl.ds(pl.multiple_of(k * q, 64), q)

        self.q0 = pl.multiple_of((2 * L.b2 + L.b1) * q, 64)
        mine = pl.ds(self.q0, q)
        near = quarter(2 * L.b2 + 1 - L.b1)
        self.u0 = pl.multiple_of(L.b2 * h, 128)
        upper = pl.ds(self.u0, h)
        lower = pl.ds(pl.multiple_of((1 - L.b2) * h, 128), h)
        ss, rs = S.rsend, S.rrecv
        out = (S.g_att, S.g_exp, S.g_con)[ch]
        self.core = remote(w.at[:, :, other], S.r1.at[ch], ss.at[ch, 0], rs.at[ch, 0], L.to(dp=L.sib))
        late = {EXP: 0, ATT: 1}.get(ch)
        self.r2 = S.r2 if late is None else S.r1.at[CON, :, late * h : late * h + h]
        self.r3 = S.r3 if late is None else S.r2.at[:, late * q : late * q + q]
        self.two = remote(w.at[:, lower, cols], self.r2, ss.at[ch, 1], rs.at[ch, 1], L.to(dp=L.p2))
        self.one = remote(w.at[:, near, cols], self.r3, ss.at[ch, 2], rs.at[ch, 2], L.to(dp=L.p1))
        self.z = [
            remote(w.at[r, mine, cols], S.r4.at[ch, NZ - 1 - r], ss.at[ch, 2 + r], rs.at[ch, 6 - r], L.to(t=L.peer(r)))
            for r in range(1, NZ)
        ]
        self.more = [
            remote(S.r4.at[ch, i], S.r5.at[ch, i], ss.at[ch, 11 + i], rs.at[ch, 11 + i], L.to(dp=m))
            for i, m in enumerate(L.more)
        ]
        own = w.at[0, mine, cols]
        self.keep = pltpu.make_async_copy(own, out.at[mine, cols], S.lsem.at[3 + ch])
        self.back_one = remote(own, out.at[mine, cols], ss.at[ch, 6], rs.at[ch, 6], L.to(dp=L.p1))
        self.back_two = remote(out.at[upper, cols], out.at[upper, cols], ss.at[ch, 7], rs.at[ch, 7], L.to(dp=L.p2))
        self.back_sib = [
            remote(own, out.at[mine, cols], ss.at[ch, 8], rs.at[ch, 8], L.to(dp=L.sib)),
            remote(out.at[near, cols], out.at[near, cols], ss.at[ch, 9], rs.at[ch, 9], L.to(dp=L.sib)),
            remote(out.at[lower, cols], out.at[lower, cols], ss.at[ch, 10], rs.at[ch, 10], L.to(dp=L.sib)),
        ]

    def start(self):
        self.core.start()

    def add(self, src, first, count):
        w, cols = self.w, self.cols
        step = self.q

        def f(i):
            r, k = i // (count // step), i % (count // step)
            at = pl.ds(first + pl.multiple_of(k * step, 64), step)
            got = src[r, pl.ds(pl.multiple_of(k * step, 64), step), :].astype(F32)
            w[r, at, cols] = (w[r, at, cols].astype(F32) + got).astype(BF)

        loop(NZ * (count // step), f)

    def merge_core(self):
        self.core.wait()
        self.add(self.S.r1.at[self.ch], 0, 2 * self.h)

    def after_core(self):
        self.merge_core()
        self.two.start()

    def after_two(self):
        self.two.wait()
        self.add(self.r2, self.u0, self.h)
        self.one.start()

    def after_one(self):
        self.one.wait()
        self.add(self.r3, self.q0, self.q)
        for k in self.z:
            k.start()

    def after_z(self):
        S, w = self.S, self.w
        for k in self.z:
            k.wait()
        mine = pl.ds(self.q0, self.q)
        v = w[0, mine, self.cols].astype(F32)
        for k in range(NZ - 1):
            v = v + S.r4[self.ch, k].astype(F32)
        for i, k in enumerate(self.more):
            S.r4[self.ch, i] = v.astype(BF)
            k.start()
            k.wait()
            v = S.r4[self.ch, i].astype(F32) + S.r5[self.ch, i].astype(F32)
        w[0, mine, self.cols] = v.astype(BF)
        self.keep.start()
        self.back_one.start()
        self.back_sib[0].start()

    def after_back_one(self):
        self.keep.wait()
        self.back_one.wait()
        self.back_two.start()
        self.back_sib[1].start()

    def after_back_two(self):
        self.back_two.wait()
        self.back_sib[2].start()

    def finish(self):
        for k in self.back_sib:
            k.wait()


class Spread:
    def __init__(self, S, L, own, out):
        self.t = L.t
        right, left = L.to(t=(L.t + 1) % NZ), L.to(t=(L.t + NZ - 1) % NZ)
        ss, rs = S.osend, S.orecv

        def block(j):
            return out.at[(L.t + j + NZ) % NZ]

        self.keep = pltpu.make_async_copy(own, out.at[L.t], S.lsem.at[6])
        self.side = [
            [remote(own if i == 0 else block(-i), block(-i), ss.at[i], rs.at[i], right) for i in range(NZ - 1)],
            [remote(own if i == 0 else block(i), block(i), ss.at[3 + i], rs.at[3 + i], left) for i in range(NZ - 1)],
        ]

    def when_sent(self, i, f):
        pl.when((self.t >= i) & (self.t < NZ - 1))(lambda: f(self.side[0][i]))
        pl.when((self.t <= NZ - 1 - i) & (self.t > 0))(lambda: f(self.side[1][i]))

    def start(self):
        self.keep.start()
        self.send(0)

    def send(self, i):
        self.when_sent(i, lambda k: k.start())

    def arrive(self, i):
        pl.when(self.t >= i + 1)(lambda: self.side[0][i].wait_recv())
        pl.when(self.t <= NZ - 2 - i)(lambda: self.side[1][i].wait_recv())

    def forward(self, i):
        self.arrive(i - 1)
        self.send(i)

    def finish(self):
        self.keep.wait()
        self.arrive(NZ - 2)
        for i in range(NZ - 1):
            self.when_sent(i, lambda k: k.wait_send())


class SmallSum:
    def __init__(self, S, L):
        self.S = S
        ss, rs = S.ssend, S.srecv
        partners = [L.sib, L.p1, L.p2] + L.more
        self.rounds = [
            remote(S.small_out.at[i], S.small_in.at[i], ss.at[i], rs.at[i], L.to(dp=p)) for i, p in enumerate(partners)
        ]
        n = len(partners)
        self.L = L
        self.z = [
            remote(S.small, S.sums.at[L.t], ss.at[n + r - 1], rs.at[n + NZ - 1 - r], L.to(t=L.peer(r)))
            for r in range(1, NZ)
        ]

    def start(self, i):
        self.S.small_out[i] = self.S.small[...]
        self.rounds[i].start()

    def after(self, i):
        self.rounds[i].wait()
        self.S.small[...] += self.S.small_in[i]
        if i + 1 < len(self.rounds):
            self.start(i + 1)
        else:
            for k in self.z:
                k.start()

    def finish(self):
        S, t = self.S, self.L.t
        for k in self.z:
            k.wait()
        S.sums[t] = S.small[...]
        total = S.sums[0] + S.sums[1] + S.sums[2] + S.sums[3]
        S.vec_out[...] = total
        w = S.d // NZ
        hidden = jnp.zeros((1, S.d), F32)
        heads = jnp.zeros((8, S.d), F32)
        for k in range(NZ):
            r = (t + NZ - k) % NZ
            hidden = hidden + S.sums[k, pl.ds(r, 1), :]
            heads = heads + pltpu.roll(S.sums[k, 8:16, :], ((NZ - r) % NZ) * w, 1)
        S.vec_out[0:1, :] = hidden
        S.vec_out[1:3, :] = heads[2:4, :]


NAMES_IN = ("tokens", "cot", "segments", "wi", "wo", "we", "wc", "qb", "vb", "eb", "ob", "g1", "s1", "g2", "s2", "cb")
NAMES_OUT = ("layers", "token_grads", "g_att", "g_exp", "g_con", "vec_out", "kept")


def layer_kernel(n_dp, names, *refs):
    S = Bag()
    for n, r in zip(names, refs):
        setattr(S, n, r)
    S.t, S.d = S.x.shape
    t, d = S.t, S.d
    n_heads, pairs = d // 64, d // 128
    S.w = [S.wbuf.at[0], S.wbuf.at[1], S.wbuf.at[2]]
    S.vec = S.table.at[pl.ds(8, 8)]
    L = Links(n_dp)

    def pool(first, n):
        return S.pool.at[pl.ds(pl.multiple_of(first, 64), n)]

    S.probs = lambda i: S.pool.at[pl.ds(pl.multiple_of(i * t, 64), t), 0:t]
    S.slope = lambda r: pool((n_heads + NZ + r) * t, t)
    spare = [S.pool.at[(n_heads + NZ + r) * t : (n_heads + NZ + r + 1) * t] for r in range(NZ)]
    S.seg_q = [spare[2].at[:, 128 * h : 128 * h + 128] for h in (0, 1)]
    S.seg_k = [spare[2].at[:, 256 + 128 * h : 384 + 128 * h] for h in (0, 1)]
    S.keys_t = [spare[3].at[128 * h : 128 * h + 128, 0:t] for h in (0, 1)]
    S.pair_s = [S.wbuf.at[EXP, h, 0:t, 0:t] for h in (0, 1)]
    S.pair_g = [S.wbuf.at[EXP, 2, 0:t, 128 * h : 128 * h + 128] for h in (0, 1)]
    S.pair_q = [S.wbuf.at[EXP, 2, 0:t, 256 + 128 * h : 384 + 128 * h] for h in (0, 1)]
    S.values_t = S.wbuf.at[EXP, 3, 0:128, 0:t]
    S.grad = S.up

    own, other = Bag(), Bag()
    own.x, own.normed, own.proj, own.heads, own.middle = S.x, S.normed, S.proj, S.heads, S.middle
    own.second, own.keep, own.active = S.second, True, lambda r: pool((n_heads + r) * t, t)
    own.weight = lambda ch, r: S.wbuf.at[ch, r]
    other.x, other.normed, other.proj, other.heads, other.middle = S.x, S.heads, S.proj, S.gheads, S.middle
    other.second, other.keep, other.active = S.branch, False, S.slope
    other.weight = lambda ch, r: S.wbuf.at[ch, r] if ch == CON else pool((ch * NZ + r) * d, d)
    S.own = own

    barrier = pltpu.get_barrier_semaphore()
    partners = [L.to(dp=p) for p in [L.sib, L.p1, L.p2] + L.more] + [L.to(t=L.peer(r)) for r in range(1, NZ)]
    for p in partners:
        pl.semaphore_signal(barrier, inc=1, device_id=p, device_id_type=MESH)
    w = d // NZ
    shards = [
        pltpu.make_async_copy(S.wi, S.w[ATT].at[0, 0 : 3 * w], S.lsem.at[0]),
        pltpu.make_async_copy(S.wo, S.w[ATT].at[0, 3 * w : 4 * w], S.lsem.at[1]),
        pltpu.make_async_copy(S.we, S.w[EXP].at[0], S.lsem.at[2]),
        pltpu.make_async_copy(S.wc, S.w[CON].at[0], S.lsem.at[7]),
    ]
    load_x = pltpu.make_async_copy(S.tokens.at[L.t], S.x, S.lsem.at[8])
    load_up = pltpu.make_async_copy(S.cot.at[L.t], S.up, S.lsem.at[9])
    for k in shards + [load_x, load_up]:
        k.start()
    save = [[pltpu.make_async_copy(S.wbuf.at[c, r], S.kept.at[c, r], S.saved.at[c, r]) for r in range(NZ)] for c in range(2)]
    reload = [
        [pltpu.make_async_copy(S.kept.at[c, r], other.weight(c, r), S.loaded.at[c, r]) for r in range(NZ)] for c in range(2)
    ]

    def every(copies, what):
        for k in copies:
            getattr(k, what)()

    bias = [
        remote(S.table.at[pl.ds(0, 8)], S.bias.at[r], S.bsend.at[r - 1], S.brecv.at[r - 1], L.to(t=L.peer(NZ - r)))
        for r in range(1, NZ)
    ]
    third = d // 3
    parts = [(ATT, w * i, w) for i in range(NZ)] + [(ch, third * i, third) for ch in (EXP, CON) for i in range(3)]
    G = [Gather(S, L, k, *part) for k, part in enumerate(parts)]
    R = [Reduce(S, L, ch) for ch in range(3)]
    tokens = Spread(S, L, S.grad, S.token_grads)
    small = SmallSum(S, L)
    put_own = pltpu.make_async_copy(S.layer, S.layers.at[L.t], S.lsem.at[10])

    def gather(k):
        n = len(G)
        if k < n:
            G[k].after_z()
            if k + 2 < n:
                G[k + 2].start()
        if 0 <= k - 1 < n:
            G[k - 1].after_one()
        if 0 <= k - 2 < n:
            G[k - 2].after_two()

    def load_other(i):
        return pltpu.make_async_copy(S.tokens.at[L.peer(i + 1)], S.x, S.lsem.at[11])

    def put_other(i):
        return pltpu.make_async_copy(S.layer, S.layers.at[L.peer(i + 1)], S.lsem.at[12])

    S.table[...] = jnp.zeros_like(S.table)
    for row, ref in ((0, S.qb), (2, S.vb), (3, S.eb)):
        S.table[row : row + 1, 0 : ref.shape[0]] = ref[...].astype(F32).reshape(1, ref.shape[0])
    for row, ref in enumerate((S.ob, S.g1, S.s1, S.g2, S.s2, S.cb)):
        S.table[8 + row : 9 + row, :] = ref[...].astype(F32).reshape(1, d)
    S.bias[0] = S.table[0:8, :]
    every(shards[:2], "wait")
    pl.semaphore_wait(barrier, len(partners))
    G[0].start()
    G[1].start()
    every(bias, "start")
    every(shards[2:], "wait")
    segment_tables(S, L.t)
    load_x.wait()
    first_norm(S, own)
    gather(0)
    every(bias, "wait")
    set_bias(S)
    gather(1)
    for c in range(3):
        gather(c + 2)
        G[c].finish()
        project(S, own, c)

    def pair(p):
        attend_pair(S, own, p)
        pl.when(p == 1)(lambda: gather(5))
        pl.when(p == 4)(lambda: gather(6))

    loop(pairs, pair)
    G[3].finish()
    every(save[ATT], "start")
    attend_out(S, own)
    load_up.wait()
    mask_upstream(S)
    gather(7)
    gather(8)
    for k in (4, 5, 6):
        G[k].finish()
    every(save[EXP], "start")
    expand_up(S, own, lambda r: pl.when(r == 2)(lambda: gather(9)))
    contract_grad(S, lambda r: pl.when(r == 2)(lambda: gather(10)))
    R[CON].start()
    G[7].finish()
    hidden_back(S, 0, third)
    G[8].finish()
    hidden_back(S, 1, third)
    R[CON].merge_core()
    gather(11)
    R[CON].two.start()
    G[9].finish()
    hidden_back(S, 2, third)

    S.layer[...] = S.middle[...].astype(BF)
    second_back(S)
    heads_back(S)
    for g in G:
        g.drain()
    for c in range(2):
        every(save[c], "wait")

    def pair_back(p):
        attend_back_pair(S, p)
        pl.when(p == 4)(R[CON].after_two)

    loop(pairs, pair_back)
    first_back(S)
    tokens.start()
    small.start(0)
    load_other(0).start()
    for c in range(2):
        every(reload[c], "start")
    expand_grad(S)
    R[EXP].start()
    R[CON].after_one()
    outproj_grad(S)
    inproj_grad(S)
    R[EXP].after_core()
    R[ATT].start()
    contract_down(S, own)
    put_own.start()

    def rounds():
        for i in range(2, 3 + len(L.more)):
            small.after(i)

    steps = {
        (0, 0): [R[ATT].after_core],
        (0, 3): [lambda: small.after(0)],
        (0, 6): [lambda: small.after(1)],
        (0, 7): [lambda: tokens.forward(1)],
        (0, 9): [R[CON].after_z],
        (1, 0): [R[EXP].after_two],
        (1, 1): [R[CON].after_back_one],
        (1, 2): [R[ATT].after_two],
        (1, 4): [R[CON].after_back_two, rounds],
        (1, 5): [R[EXP].after_one],
        (1, 8): [R[ATT].after_one, lambda: tokens.forward(2)],
        (2, 2): [R[EXP].after_z],
        (2, 4): [R[EXP].after_back_one],
        (2, 6): [R[ATT].after_z, R[EXP].after_back_two],
        (2, 5): [small.finish],
        (2, 8): [R[ATT].after_back_one],
        (2, 9): [R[ATT].after_back_two],
    }

    def at(i, q):
        for (si, sq), fs in steps.items():
            if isinstance(q, int):
                if sq == q:
                    pl.when(i == si)(lambda fs=fs: [f() for f in fs] and None)
            elif 1 <= sq <= pairs:
                pl.when((i == si) & (q == sq))(lambda fs=fs: [f() for f in fs] and None)

    def forward_other(i):
        load_other(i).wait()
        pl.when(i == 0)(lambda: every(reload[ATT], "wait"))
        segment_tables(S, L.peer(i + 1))
        first_norm(S, other)
        for c in range(3):
            project(S, other, c)
        at(i, 0)

        def pair_other(p):
            attend_pair(S, other, p)
            at(i, p + 1)

        loop(pairs, pair_other)
        attend_out(S, other)
        pl.when(i < NZ - 2)(lambda: load_other(i + 1).start())
        at(i, 7)
        pl.when(i == 0)(lambda: every(reload[EXP], "wait"))
        expand_up(S, other)
        at(i, 8)
        pl.when(i > 0)(lambda: put_other(i - 1).wait())
        pl.when(i == 0)(put_own.wait)
        contract_down(S, other)
        put_other(i).start()
        at(i, 9)

    loop(NZ - 1, forward_other)
    put_other(NZ - 2).wait()
    for r in R:
        r.finish()
    tokens.finish()


def run_layer(n_dp, tokens, cot, segments, wi, wo, we, wc, *vectors):
    _, t, d = tokens.shape
    more = max(n_dp.bit_length() - 1 - 3, 0)
    spare = max(more, 1)
    any_, vmem = pl.BlockSpec(memory_space=pl.ANY), pl.BlockSpec(memory_space=pltpu.VMEM)
    V, DMA = pltpu.VMEM, pltpu.SemaphoreType.DMA
    scratch = dict(
        x=V((t, d), BF),
        up=V((t, d), BF),
        normed=V((t, d), BF),
        proj=V((t, 3 * d), BF),
        heads=V((t, d), BF),
        pool=V(((d // 64 + 2 * NZ) * t, d), BF),
        middle=V((t, d), F32),
        second=V((t, d), BF),
        branch=V((t, d), BF),
        gheads=V((t, d), BF),
        seg_col=V((t, 128), F32),
        sums=V((NZ, 16, d), F32),
        layer=V((t, d), BF),
        inv_sum=V((t, 128), F32),
        wbuf=V((3, NZ, d, d), BF),
        con_grad=V((NZ, d, d), BF),
        table=V((16, d), F32),
        bias=V((NZ, 8, d), F32),
        qkv_bias=V((8, d), F32),
        small=V((16, d), F32),
        small_in=V((3 + more, 16, d), F32),
        small_out=V((3 + more, 16, d), F32),
        r1=V((3, NZ, d, d // 2), BF),
        r2=V((NZ, d // 2, d // 2), BF),
        r3=V((NZ, d // 4, d // 2), BF),
        r4=V((3, NZ - 1, d // 4, d // 2), BF),
        r5=V((3, spare, d // 4 if more else 16, d // 2), BF),
        lsem=DMA((13,)),
        gsend=DMA((10, 8)),
        grecv=DMA((10, 8)),
        rsend=DMA((3, 11 + spare)),
        rrecv=DMA((3, 11 + spare)),
        osend=DMA((6,)),
        orecv=DMA((6,)),
        saved=DMA((2, NZ)),
        loaded=DMA((2, NZ)),
        ssend=DMA((6 + more,)),
        srecv=DMA((6 + more,)),
        bsend=DMA((3,)),
        brecv=DMA((3,)),
    )
    names = NAMES_IN + NAMES_OUT + tuple(scratch)
    out_shape = [
        jax.ShapeDtypeStruct((NZ, t, d), BF),
        jax.ShapeDtypeStruct((NZ, t, d), BF),
        jax.ShapeDtypeStruct((d, d), BF),
        jax.ShapeDtypeStruct((d, d), BF),
        jax.ShapeDtypeStruct((d, d), BF),
        jax.ShapeDtypeStruct((16, d), F32),
        jax.ShapeDtypeStruct((2, NZ, d, d), BF),
    ]
    return pl.pallas_call(
        functools.partial(layer_kernel, n_dp, names),
        out_shape=out_shape,
        in_specs=[any_, any_, vmem, any_, any_, any_, any_] + [vmem] * len(vectors),
        out_specs=[any_] * 5 + [vmem, any_],
        scratch_shapes=list(scratch.values()),
        compiler_params=pltpu.CompilerParams(
            collective_id=0, has_side_effects=True, vmem_limit_bytes=63 << 20
        ),
        name="layer",
    )(tokens, cot, segments, wi, wo, we, wc, *vectors)


def local(
    n_dp,
    tokens,
    segments,
    cotangent,
    inproj,
    querybias,
    valuebias,
    outproj,
    outbias,
    gainone,
    shiftone,
    gaintwo,
    shifttwo,
    expand,
    expandbias,
    contract,
    contractbias,
):
    _, t, d = tokens.shape
    w = d // NZ
    wi = inproj.transpose(1, 2, 0).reshape(3 * w, d)
    vectors = (querybias, valuebias, expandbias, outbias, gainone, shiftone, gaintwo, shifttwo, contractbias)
    layers, token_grads, g_att, g_exp, g_con, vec, _ = run_layer(n_dp, tokens, cotangent, segments, wi, outproj, expand, contract, *vectors)
    return (
        layers,
        token_grads,
        g_att[: 3 * w].astype(F32).reshape(3, w, d).transpose(2, 0, 1),
        vec[1, :w],
        vec[2, :w],
        g_att[3 * w :].astype(F32),
        vec[5],
        vec[6],
        vec[7],
        vec[8],
        vec[9],
        g_exp.astype(F32),
        vec[0],
        g_con.astype(F32),
        vec[4],
    )


def solution(mesh):
    in_specs = (
        P("dp", None, None),
        P("dp", None),
        P("dp", None, None),
        P(None, None, "tensor"),
        P("tensor"),
        P("tensor"),
        P("tensor", None),
        P(),
        P(),
        P(),
        P(),
        P(),
        P(None, "tensor"),
        P("tensor"),
        P("tensor", None),
        P(),
    )
    out_specs = (
        P("dp", None, None),
        P("dp", None, None),
        P(None, None, "tensor"),
        P("tensor"),
        P("tensor"),
        P("tensor", None),
        P(),
        P(),
        P(),
        P(),
        P(),
        P(None, "tensor"),
        P("tensor"),
        P("tensor", None),
        P(),
    )
    return jax.shard_map(
        functools.partial(local, mesh.shape["dp"]),
        mesh=mesh,
        in_specs=in_specs,
        out_specs=out_specs,
        check_vma=False,
    )
```

```python
import functools

import jax
import jax.numpy as jnp
from jax import lax
from jax.experimental import pallas as pl
from jax.experimental.pallas import tpu as pltpu
from jax.sharding import PartitionSpec as P

BF = jnp.bfloat16
F32 = jnp.float32
EPSILON = 1e-06
LOG2E = 1.4426950408889634
ROOT_HALF = 0.7071067811865476
INV_ROOT_TWO_PI = 0.3989422804014327
MESH = pl.DeviceIdType.MESH
RT = 192
APART = 2.0**100
NZ = 4
OUT_BIAS, GAIN_ONE, SHIFT_ONE, GAIN_TWO, SHIFT_TWO, CONTRACT_BIAS = range(6)
ATT, EXP, CON = range(3)


def nt(a, b):
    return lax.dot_general(a, b, (((1,), (1,)), ((), ())), preferred_element_type=F32)


def nn(a, b):
    return lax.dot_general(a, b, (((1,), (0,)), ((), ())), preferred_element_type=F32)


def tn(a, b):
    return lax.dot_general(a, b, (((0,), (0,)), ((), ())), preferred_element_type=F32)


def at128(i):
    return pl.ds(pl.multiple_of(i * 128, 128), 128)


def at256(i):
    return pl.ds(pl.multiple_of(i * 256, 256), 256)


def rows(i):
    return pl.ds(pl.multiple_of(i * RT, RT), RT)


def loop(n, f):
    def body(i, carry):
        f(i)
        return carry

    lax.fori_loop(0, n, body, 0)


def standardize(v):
    mu = jnp.mean(v, -1, keepdims=True)
    c = v - mu
    inv = lax.rsqrt(jnp.mean(c * c, -1, keepdims=True) + EPSILON)
    return c * inv, inv


def norm_back(z, unit, inv, gain):
    s = z * gain
    a = jnp.mean(s, -1, keepdims=True)
    b = jnp.mean(s * unit, -1, keepdims=True)
    return inv * (s - a - unit * b)


def head_lanes(shape, h):
    lane = lax.broadcasted_iota(jnp.int32, shape, 1)
    return (lane < 64) if h == 0 else (lane >= 64)


class Bag:
    pass


def segment_column(S, t):
    row = S.segments[pl.ds(t, 1), :].astype(F32)
    S.seg_col[...] = jnp.broadcast_to(row, (128, S.t)).T


def segment_tables(S, t):
    segment_column(S, t)
    lane = lax.broadcasted_iota(jnp.int32, (S.t, 128), 1)
    ids = S.seg_col[...].astype(jnp.int32)
    for h in (0, 1):
        at = lane - (64 if h == 0 else 0)
        same = at == ids
        S.seg_q[h][...] = jnp.where(same, 1.0, 0.0).astype(BF)
        S.seg_k[h][...] = jnp.where((at >= 0) & (at < 8) & (~same), -APART, 0.0).astype(BF)


def first_norm(S, B):
    u, _ = standardize(B.x[...].astype(F32))
    B.normed[...] = (
        u * S.vec[GAIN_ONE : GAIN_ONE + 1, :] + S.vec[SHIFT_ONE : SHIFT_ONE + 1, :]
    ).astype(BF)


def set_bias(S):
    placed = S.bias[0]
    for r in range(1, NZ):
        placed = placed + pltpu.roll(S.bias[r], r * (S.d // NZ), 1)
    S.qkv_bias[...] = placed


def part_matrix(S, B, c):
    w = S.d // NZ
    return jnp.concatenate([B.weight(ATT, r)[c * w : (c + 1) * w, :] for r in range(NZ)], 0)


def project(S, B, c):
    y = nt(B.normed[...], part_matrix(S, B, c)) + S.qkv_bias[c : c + 1, :]
    B.proj[:, c * S.d : (c + 1) * S.d] = y.astype(BF)


def attend_pair(S, B, p):
    n = S.d // 128
    k2 = B.proj[:, at128(n + p)]
    v2 = B.proj[:, at128(2 * n + p)]
    q2 = B.proj[:, at128(p)]
    lane = lax.broadcasted_iota(jnp.int32, (S.t, 128), 1)
    outs, sums = [], []
    for h in (0, 1):
        own = head_lanes(q2.shape, h)
        one = lane == (64 if h == 0 else 0)
        flat = S.keys_t[h]
        flat[...] = jnp.where(own, k2, S.seg_k[h][...]).T
        s = nn(jnp.where(own, q2, S.seg_q[h][...]), flat[...])
        e = jnp.exp2((s - jnp.max(s, -1, keepdims=True)) * (0.125 * LOG2E)).astype(BF)
        if B.keep:
            S.probs(2 * p + h)[...] = e
        o = nn(e, jnp.where(own, v2, jnp.where(one, 1.0, 0.0).astype(BF)))
        at = 64 if h == 0 else 0
        sums.append(1.0 / o[:, at : at + 1])
        outs.append(o)
    first = head_lanes(outs[0].shape, 0)
    scale = jnp.where(first, sums[0], sums[1])
    if B.keep:
        kept = jnp.where(lane == 2 * p, sums[0], S.inv_sum[...])
        S.inv_sum[...] = jnp.where(lane == 2 * p + 1, sums[1], kept)
    B.heads[:, at128(p)] = (jnp.where(first, outs[0], outs[1]) * scale).astype(BF)


def attend_out(S, B):
    m = B.x[...].astype(F32) + nn(B.heads[...], part_matrix(S, B, 3)) + S.vec[OUT_BIAS : OUT_BIAS + 1, :]
    B.middle[...] = m
    u, _ = standardize(m)
    B.second[...] = (
        u * S.vec[GAIN_TWO : GAIN_TWO + 1, :] + S.vec[SHIFT_TWO : SHIFT_TWO + 1, :]
    ).astype(BF)


def expand_up(S, B, done=lambda r: None):
    def g(r):
        w = B.weight(EXP, r)
        for j in range(S.d // 256):
            c = slice(256 * j, 256 * j + 256)
            h = nn(B.second[...], w[:, c]) + S.bias[r, 3:4, c]
            cdf = 0.5 + 0.5 * lax.erf(h * ROOT_HALF)
            B.active(r)[:, c] = (h * cdf).astype(BF)
            if B.keep:
                S.slope(r)[:, c] = (cdf + h * jnp.exp2(h * h * (-0.5 * LOG2E)) * INV_ROOT_TWO_PI).astype(BF)
        done(r)

    loop(NZ, g)


def contract_down(S, B):
    a = (S.layer if B.keep else B.middle)[...].astype(F32) + S.vec[CONTRACT_BIAS : CONTRACT_BIAS + 1, :]
    for r in range(NZ):
        a = a + nn(B.active(r)[...], B.weight(CON, r)[...])
    S.layer[...] = a.astype(BF)


def mask_upstream(S):
    S.small[...] = jnp.zeros_like(S.small)
    g = jnp.where(S.seg_col[:, 0:1] > 0.0, S.up[...].astype(F32), 0.0)
    S.up[...] = g.astype(BF)
    S.small[4:5, :] = jnp.sum(g, 0, keepdims=True)


def hidden_back(S, j, n):
    c = slice(n * j, n * j + n)

    def f(r):
        gh = (nt(S.up[...], S.wbuf[CON, r, c, :]) * S.slope(r)[:, c].astype(F32)).astype(BF)
        S.slope(r)[:, c] = gh
        S.small[pl.ds(r, 1), c] = jnp.sum(gh.astype(F32), 0, keepdims=True)

    loop(NZ, f)


def contract_grad(S, done):
    def f(r):
        S.con_grad[r] = tn(S.own.active(r)[...], S.up[...]).astype(BF)
        done(r)

    loop(NZ, f)


def second_back(S):
    n = S.t // 2
    for k in (8, 9, 5):
        S.small[k : k + 1, :] = jnp.zeros((1, S.d), F32)

    def f(i):
        at = pl.ds(pl.multiple_of(i * n, 32), n)
        gs = nt(S.slope(0)[at, :], S.w[EXP][0])
        for r in range(1, NZ):
            gs = gs + nt(S.slope(r)[at, :], S.w[EXP][r])
        u, inv = standardize(S.middle[at, :])
        gm = S.up[at, :].astype(F32) + norm_back(gs, u, inv, S.vec[GAIN_TWO : GAIN_TWO + 1, :])
        S.middle[at, :] = gm
        gb = gm.astype(BF)
        S.branch[at, :] = gb
        S.small[8:9, :] += jnp.sum(gs * u, 0, keepdims=True)
        S.small[9:10, :] += jnp.sum(gs, 0, keepdims=True)
        S.small[5:6, :] += jnp.sum(gb.astype(F32), 0, keepdims=True)

    loop(2, f)


def expand_grad(S):
    def f(r):
        S.w[EXP][r] = tn(S.second[...], S.slope(r)[...]).astype(BF)

    loop(NZ, f)


def heads_back(S):
    S.gheads[...] = nt(S.branch[...], part_matrix(S, S.own, 3)).astype(BF)


def store_part(S, c, v):
    w = S.d // NZ
    for r in range(NZ):
        S.w[ATT][r, c * w : (c + 1) * w, :] = v[r * w : (r + 1) * w, :]


def outproj_grad(S):
    store_part(S, 3, tn(S.heads[...], S.branch[...]).astype(BF))


def attend_back_pair(S, p):
    n = S.d // 128
    q2 = S.proj[:, at128(p)]
    k2 = S.proj[:, at128(n + p)]
    v2 = S.proj[:, at128(2 * n + p)]
    lane = lax.broadcasted_iota(jnp.int32, (S.t, 128), 1)
    values = S.values_t
    values[...] = v2.T
    kept = S.inv_sum[...]
    scale = [jnp.sum(jnp.where(lane == 2 * p + h, kept, 0.0), -1, keepdims=True) for h in (0, 1)]
    first = head_lanes(q2.shape, 0)
    g2 = (S.gheads[:, at128(p)].astype(F32) * jnp.where(first, scale[0], scale[1])).astype(BF)
    od = g2.astype(F32) * S.heads[:, at128(p)].astype(F32)
    none = jnp.zeros_like(q2)
    dq = None
    for h in (0, 1):
        own = head_lanes(q2.shape, h)
        gm = jnp.where(own, g2, none)
        S.pair_g[h][...] = gm
        S.pair_q[h][...] = jnp.where(own, q2, none)
        dot_sum = jnp.sum(jnp.where(own, od, 0.0), -1, keepdims=True)
        ds = (S.probs(2 * p + h)[...].astype(F32) * (nn(gm, values[...]) - dot_sum)).astype(BF)
        S.pair_s[h][...] = ds
        y = nn(ds, jnp.where(own, k2, none))
        dq = y if dq is None else dq + y
    S.proj[:, at128(p)] = (dq * 0.125).astype(BF)
    dk = tn(S.pair_q[0][...], S.pair_s[0][...]) + tn(S.pair_q[1][...], S.pair_s[1][...])
    dv = tn(S.pair_g[0][...], S.probs(2 * p)[...]) + tn(S.pair_g[1][...], S.probs(2 * p + 1)[...])
    S.proj[:, at128(n + p)] = (dk.T * 0.125).astype(BF)
    S.proj[:, at128(2 * n + p)] = dv.T.astype(BF)


def first_back(S):
    n = S.t // 2
    for k in (6, 7, 10, 11):
        S.small[k : k + 1, :] = jnp.zeros((1, S.d), F32)

    def f(i):
        at = pl.ds(pl.multiple_of(i * n, 32), n)
        gf = None
        for c in range(3):
            y = nn(S.proj[at, c * S.d : (c + 1) * S.d], part_matrix(S, S.own, c))
            gf = y if gf is None else gf + y
        u, inv = standardize(S.x[at, :].astype(F32))
        S.grad[at, :] = (S.middle[at, :] + norm_back(gf, u, inv, S.vec[GAIN_ONE : GAIN_ONE + 1, :])).astype(BF)
        S.small[6:7, :] += jnp.sum(gf * u, 0, keepdims=True)
        S.small[7:8, :] += jnp.sum(gf, 0, keepdims=True)
        S.small[10:11, :] += jnp.sum(S.proj[at, 0 : S.d].astype(F32), 0, keepdims=True)
        S.small[11:12, :] += jnp.sum(S.proj[at, 2 * S.d : 3 * S.d].astype(F32), 0, keepdims=True)

    loop(2, f)


def inproj_grad(S):
    for c in range(3):
        store_part(S, c, tn(S.proj[:, c * S.d : (c + 1) * S.d], S.normed[...]).astype(BF))


class Links:
    def __init__(self, n_dp):
        self.dp = lax.axis_index("dp")
        self.t = lax.axis_index("tensor")
        self.c = self.dp % 2
        bx = (self.dp // 2) % 2
        by = (self.dp // 4) % 2
        self.b1 = bx + self.c * (by - bx)
        self.b2 = by + self.c * (bx - by)
        self.sib = self.dp + 1 - 2 * self.c
        self.p1 = self.dp + (1 - 2 * self.b1) * (2 + 2 * self.c)
        self.p2 = self.dp + (1 - 2 * self.b2) * (4 - 2 * self.c)
        self.more = []
        step = 8
        while step < n_dp:
            self.more.append(self.dp + (1 - 2 * ((self.dp // step) % 2)) * step)
            step *= 2

    def peer(self, r):
        return (self.t + r) % NZ

    def to(self, dp=None, t=None):
        return {"dp": self.dp if dp is None else dp, "tensor": self.t if t is None else t}


def remote(src, dst, ssem, rsem, to):
    return pltpu.make_async_remote_copy(
        src_ref=src, dst_ref=dst, send_sem=ssem, recv_sem=rsem, device_id=to, device_id_type=MESH
    )


class Gather:
    def __init__(self, S, L, k, chunk, base, n):
        d = S.d
        ch = k
        q, h = n // 4, d // 2
        cols = pl.ds(pl.multiple_of(L.c * h, 128), h)
        w = S.w[chunk]

        def quarter(k):
            return pl.ds(base + pl.multiple_of(k * q, 16), q)

        mine = quarter(2 * L.b2 + L.b1)
        near = quarter(2 * L.b2 + 1 - L.b1)
        upper = pl.ds(base + pl.multiple_of(L.b2 * 2 * q, 16), 2 * q)
        lower = pl.ds(base + pl.multiple_of((1 - L.b2) * 2 * q, 16), 2 * q)
        ss, rs = S.gsend, S.grecv
        src = w.at[0]
        self.z = [
            remote(src.at[mine, cols], w.at[r, mine, cols], ss.at[ch, r - 1], rs.at[ch, r - 1], L.to(t=L.peer(NZ - r)))
            for r in range(1, NZ)
        ]
        far = pl.ds(1, NZ - 1)
        self.one = remote(w.at[far, mine, cols], w.at[far, mine, cols], ss.at[ch, 3], rs.at[ch, 3], L.to(dp=L.p1))
        self.two = remote(w.at[far, upper, cols], w.at[far, upper, cols], ss.at[ch, 4], rs.at[ch, 4], L.to(dp=L.p2))
        self.sib = [
            remote(w.at[far, k, cols], w.at[far, k, cols], ss.at[ch, 5 + i], rs.at[ch, 5 + i], L.to(dp=L.sib))
            for i, k in enumerate((mine, near, lower))
        ]

    def start(self):
        for k in self.z:
            k.start()

    def after_z(self):
        for k in self.z:
            k.wait_recv()
        self.one.start()
        self.sib[0].start()

    def after_one(self):
        self.one.wait_recv()
        self.two.start()
        self.sib[1].start()

    def after_two(self):
        self.two.wait_recv()
        self.sib[2].start()

    def finish(self):
        for k in self.sib:
            k.wait_recv()

    def drain(self):
        for k in self.z + [self.one, self.two] + self.sib:
            k.wait_send()


class Reduce:
    def __init__(self, S, L, ch):
        d = S.d
        q, h = d // 4, d // 2
        self.S, self.L, self.ch, self.q, self.h = S, L, ch, q, h
        w = S.con_grad if ch == CON else S.w[ch]
        self.w = w
        self.c0 = pl.multiple_of(L.c * h, 128)
        cols = pl.ds(self.c0, h)
        other = pl.ds(pl.multiple_of((1 - L.c) * h, 128), h)
        self.cols = cols

        def quarter(k):
            return pl.ds(pl.multiple_of(k * q, 64), q)

        self.q0 = pl.multiple_of((2 * L.b2 + L.b1) * q, 64)
        mine = pl.ds(self.q0, q)
        near = quarter(2 * L.b2 + 1 - L.b1)
        self.u0 = pl.multiple_of(L.b2 * h, 128)
        upper = pl.ds(self.u0, h)
        lower = pl.ds(pl.multiple_of((1 - L.b2) * h, 128), h)
        ss, rs = S.rsend, S.rrecv
        out = (S.g_att, S.g_exp, S.g_con)[ch]
        self.core = remote(w.at[:, :, other], S.r1.at[ch], ss.at[ch, 0], rs.at[ch, 0], L.to(dp=L.sib))
        late = {EXP: 0, ATT: 1}.get(ch)
        self.r2 = S.r2 if late is None else S.r1.at[CON, :, late * h : late * h + h]
        self.r3 = S.r3 if late is None else S.r2.at[:, late * q : late * q + q]
        self.two = remote(w.at[:, lower, cols], self.r2, ss.at[ch, 1], rs.at[ch, 1], L.to(dp=L.p2))
        self.one = remote(w.at[:, near, cols], self.r3, ss.at[ch, 2], rs.at[ch, 2], L.to(dp=L.p1))
        self.z = [
            remote(w.at[r, mine, cols], S.r4.at[ch, NZ - 1 - r], ss.at[ch, 2 + r], rs.at[ch, 6 - r], L.to(t=L.peer(r)))
            for r in range(1, NZ)
        ]
        self.more = [
            remote(S.r4.at[ch, i], S.r5.at[ch, i], ss.at[ch, 11 + i], rs.at[ch, 11 + i], L.to(dp=m))
            for i, m in enumerate(L.more)
        ]
        own = w.at[0, mine, cols]
        self.keep = pltpu.make_async_copy(own, out.at[mine, cols], S.lsem.at[3 + ch])
        self.back_one = remote(own, out.at[mine, cols], ss.at[ch, 6], rs.at[ch, 6], L.to(dp=L.p1))
        self.back_two = remote(out.at[upper, cols], out.at[upper, cols], ss.at[ch, 7], rs.at[ch, 7], L.to(dp=L.p2))
        self.back_sib = [
            remote(own, out.at[mine, cols], ss.at[ch, 8], rs.at[ch, 8], L.to(dp=L.sib)),
            remote(out.at[near, cols], out.at[near, cols], ss.at[ch, 9], rs.at[ch, 9], L.to(dp=L.sib)),
            remote(out.at[lower, cols], out.at[lower, cols], ss.at[ch, 10], rs.at[ch, 10], L.to(dp=L.sib)),
        ]

    def start(self):
        self.core.start()

    def add(self, src, first, count):
        w, cols = self.w, self.cols
        step = self.q

        def f(i):
            r, k = i // (count // step), i % (count // step)
            at = pl.ds(first + pl.multiple_of(k * step, 64), step)
            got = src[r, pl.ds(pl.multiple_of(k * step, 64), step), :].astype(F32)
            w[r, at, cols] = (w[r, at, cols].astype(F32) + got).astype(BF)

        loop(NZ * (count // step), f)

    def merge_core(self):
        self.core.wait()
        self.add(self.S.r1.at[self.ch], 0, 2 * self.h)

    def after_core(self):
        self.merge_core()
        self.two.start()

    def after_two(self):
        self.two.wait()
        self.add(self.r2, self.u0, self.h)
        self.one.start()

    def after_one(self):
        self.one.wait()
        self.add(self.r3, self.q0, self.q)
        for k in self.z:
            k.start()

    def after_z(self):
        S, w = self.S, self.w
        for k in self.z:
            k.wait()
        mine = pl.ds(self.q0, self.q)
        v = w[0, mine, self.cols].astype(F32)
        for k in range(NZ - 1):
            v = v + S.r4[self.ch, k].astype(F32)
        for i, k in enumerate(self.more):
            S.r4[self.ch, i] = v.astype(BF)
            k.start()
            k.wait()
            v = S.r4[self.ch, i].astype(F32) + S.r5[self.ch, i].astype(F32)
        w[0, mine, self.cols] = v.astype(BF)
        self.keep.start()
        self.back_one.start()
        self.back_sib[0].start()

    def after_back_one(self):
        self.keep.wait()
        self.back_one.wait()
        self.back_two.start()
        self.back_sib[1].start()

    def after_back_two(self):
        self.back_two.wait()
        self.back_sib[2].start()

    def finish(self):
        for k in self.back_sib:
            k.wait()


class Spread:
    def __init__(self, S, L, own, out):
        self.t = L.t
        right, left = L.to(t=(L.t + 1) % NZ), L.to(t=(L.t + NZ - 1) % NZ)
        ss, rs = S.osend, S.orecv

        def block(j):
            return out.at[(L.t + j + NZ) % NZ]

        self.keep = pltpu.make_async_copy(own, out.at[L.t], S.lsem.at[6])
        self.side = [
            [remote(own if i == 0 else block(-i), block(-i), ss.at[i], rs.at[i], right) for i in range(NZ - 1)],
            [remote(own if i == 0 else block(i), block(i), ss.at[3 + i], rs.at[3 + i], left) for i in range(NZ - 1)],
        ]

    def when_sent(self, i, f):
        pl.when((self.t >= i) & (self.t < NZ - 1))(lambda: f(self.side[0][i]))
        pl.when((self.t <= NZ - 1 - i) & (self.t > 0))(lambda: f(self.side[1][i]))

    def start(self):
        self.keep.start()
        self.send(0)

    def send(self, i):
        self.when_sent(i, lambda k: k.start())

    def arrive(self, i):
        pl.when(self.t >= i + 1)(lambda: self.side[0][i].wait_recv())
        pl.when(self.t <= NZ - 2 - i)(lambda: self.side[1][i].wait_recv())

    def forward(self, i):
        self.arrive(i - 1)
        self.send(i)

    def finish(self):
        self.keep.wait()
        self.arrive(NZ - 2)
        for i in range(NZ - 1):
            self.when_sent(i, lambda k: k.wait_send())


class SmallSum:
    def __init__(self, S, L):
        self.S = S
        ss, rs = S.ssend, S.srecv
        partners = [L.sib, L.p1, L.p2] + L.more
        self.rounds = [
            remote(S.small_out.at[i], S.small_in.at[i], ss.at[i], rs.at[i], L.to(dp=p)) for i, p in enumerate(partners)
        ]
        n = len(partners)
        self.L = L
        self.z = [
            remote(S.small, S.sums.at[L.t], ss.at[n + r - 1], rs.at[n + NZ - 1 - r], L.to(t=L.peer(r)))
            for r in range(1, NZ)
        ]

    def start(self, i):
        self.S.small_out[i] = self.S.small[...]
        self.rounds[i].start()

    def after(self, i):
        self.rounds[i].wait()
        self.S.small[...] += self.S.small_in[i]
        if i + 1 < len(self.rounds):
            self.start(i + 1)
        else:
            for k in self.z:
                k.start()

    def finish(self):
        S, t = self.S, self.L.t
        for k in self.z:
            k.wait()
        S.sums[t] = S.small[...]
        total = S.sums[0] + S.sums[1] + S.sums[2] + S.sums[3]
        S.vec_out[...] = total
        w = S.d // NZ
        hidden = jnp.zeros((1, S.d), F32)
        heads = jnp.zeros((8, S.d), F32)
        for k in range(NZ):
            r = (t + NZ - k) % NZ
            hidden = hidden + S.sums[k, pl.ds(r, 1), :]
            heads = heads + pltpu.roll(S.sums[k, 8:16, :], ((NZ - r) % NZ) * w, 1)
        S.vec_out[0:1, :] = hidden
        S.vec_out[1:3, :] = heads[2:4, :]


NAMES_IN = ("tokens", "cot", "segments", "wi", "wo", "we", "wc", "qb", "vb", "eb", "ob", "g1", "s1", "g2", "s2", "cb")
NAMES_OUT = ("layers", "token_grads", "g_att", "g_exp", "g_con", "vec_out", "kept")


def layer_kernel(n_dp, names, *refs):
    S = Bag()
    for n, r in zip(names, refs):
        setattr(S, n, r)
    S.t, S.d = S.x.shape
    t, d = S.t, S.d
    n_heads, pairs = d // 64, d // 128
    S.w = [S.wbuf.at[0], S.wbuf.at[1], S.wbuf.at[2]]
    S.vec = S.table.at[pl.ds(8, 8)]
    L = Links(n_dp)

    def pool(first, n):
        return S.pool.at[pl.ds(pl.multiple_of(first, 64), n)]

    S.probs = lambda i: S.pool.at[pl.ds(pl.multiple_of(i * t, 64), t), 0:t]
    S.slope = lambda r: pool((n_heads + NZ + r) * t, t)
    spare = [S.pool.at[(n_heads + NZ + r) * t : (n_heads + NZ + r + 1) * t] for r in range(NZ)]
    S.seg_q = [spare[2].at[:, 128 * h : 128 * h + 128] for h in (0, 1)]
    S.seg_k = [spare[2].at[:, 256 + 128 * h : 384 + 128 * h] for h in (0, 1)]
    S.keys_t = [spare[3].at[128 * h : 128 * h + 128, 0:t] for h in (0, 1)]
    S.pair_s = [S.wbuf.at[EXP, h, 0:t, 0:t] for h in (0, 1)]
    S.pair_g = [S.wbuf.at[EXP, 2, 0:t, 128 * h : 128 * h + 128] for h in (0, 1)]
    S.pair_q = [S.wbuf.at[EXP, 2, 0:t, 256 + 128 * h : 384 + 128 * h] for h in (0, 1)]
    S.values_t = S.wbuf.at[EXP, 3, 0:128, 0:t]
    S.grad = S.up

    own, other = Bag(), Bag()
    own.x, own.normed, own.proj, own.heads, own.middle = S.x, S.normed, S.proj, S.heads, S.middle
    own.second, own.keep, own.active = S.second, True, lambda r: pool((n_heads + r) * t, t)
    own.weight = lambda ch, r: S.wbuf.at[ch, r]
    other.x, other.normed, other.proj, other.heads, other.middle = S.x, S.heads, S.proj, S.gheads, S.middle
    other.second, other.keep, other.active = S.branch, False, S.slope
    other.weight = lambda ch, r: S.wbuf.at[ch, r] if ch == CON else pool((ch * NZ + r) * d, d)
    S.own = own

    barrier = pltpu.get_barrier_semaphore()
    partners = [L.to(dp=p) for p in [L.sib, L.p1, L.p2] + L.more] + [L.to(t=L.peer(r)) for r in range(1, NZ)]
    for p in partners:
        pl.semaphore_signal(barrier, inc=1, device_id=p, device_id_type=MESH)
    w = d // NZ
    shards = [
        pltpu.make_async_copy(S.wi, S.w[ATT].at[0, 0 : 3 * w], S.lsem.at[0]),
        pltpu.make_async_copy(S.wo, S.w[ATT].at[0, 3 * w : 4 * w], S.lsem.at[1]),
        pltpu.make_async_copy(S.we, S.w[EXP].at[0], S.lsem.at[2]),
        pltpu.make_async_copy(S.wc, S.w[CON].at[0], S.lsem.at[7]),
    ]
    load_x = pltpu.make_async_copy(S.tokens.at[L.t], S.x, S.lsem.at[8])
    load_up = pltpu.make_async_copy(S.cot.at[L.t], S.up, S.lsem.at[9])
    for k in shards + [load_x, load_up]:
        k.start()
    save = [[pltpu.make_async_copy(S.wbuf.at[c, r], S.kept.at[c, r], S.saved.at[c, r]) for r in range(NZ)] for c in range(2)]
    reload = [
        [pltpu.make_async_copy(S.kept.at[c, r], other.weight(c, r), S.loaded.at[c, r]) for r in range(NZ)] for c in range(2)
    ]

    def every(copies, what):
        for k in copies:
            getattr(k, what)()

    bias = [
        remote(S.table.at[pl.ds(0, 8)], S.bias.at[r], S.bsend.at[r - 1], S.brecv.at[r - 1], L.to(t=L.peer(NZ - r)))
        for r in range(1, NZ)
    ]
    third = d // 3
    parts = [(ATT, w * i, w) for i in range(NZ)] + [(ch, third * i, third) for ch in (EXP, CON) for i in range(3)]
    G = [Gather(S, L, k, *part) for k, part in enumerate(parts)]
    R = [Reduce(S, L, ch) for ch in range(3)]
    tokens = Spread(S, L, S.grad, S.token_grads)
    small = SmallSum(S, L)
    put_own = pltpu.make_async_copy(S.layer, S.layers.at[L.t], S.lsem.at[10])

    def gather(k):
        n = len(G)
        if k < n:
            G[k].after_z()
            if k + 2 < n:
                G[k + 2].start()
        if 0 <= k - 1 < n:
            G[k - 1].after_one()
        if 0 <= k - 2 < n:
            G[k - 2].after_two()

    def load_other(i):
        return pltpu.make_async_copy(S.tokens.at[L.peer(i + 1)], S.x, S.lsem.at[11])

    def put_other(i):
        return pltpu.make_async_copy(S.layer, S.layers.at[L.peer(i + 1)], S.lsem.at[12])

    S.table[...] = jnp.zeros_like(S.table)
    for row, ref in ((0, S.qb), (2, S.vb), (3, S.eb)):
        S.table[row : row + 1, 0 : ref.shape[0]] = ref[...].astype(F32).reshape(1, ref.shape[0])
    for row, ref in enumerate((S.ob, S.g1, S.s1, S.g2, S.s2, S.cb)):
        S.table[8 + row : 9 + row, :] = ref[...].astype(F32).reshape(1, d)
    S.bias[0] = S.table[0:8, :]
    every(shards[:2], "wait")
    pl.semaphore_wait(barrier, len(partners))
    G[0].start()
    G[1].start()
    every(bias, "start")
    every(shards[2:], "wait")
    segment_tables(S, L.t)
    load_x.wait()
    first_norm(S, own)
    gather(0)
    every(bias, "wait")
    set_bias(S)
    gather(1)
    for c in range(3):
        gather(c + 2)
        G[c].finish()
        project(S, own, c)

    def pair(p):
        attend_pair(S, own, p)
        pl.when(p == 1)(lambda: gather(5))
        pl.when(p == 4)(lambda: gather(6))

    loop(pairs, pair)
    G[3].finish()
    every(save[ATT], "start")
    attend_out(S, own)
    load_up.wait()
    mask_upstream(S)
    gather(7)
    gather(8)
    for k in (4, 5, 6):
        G[k].finish()
    every(save[EXP], "start")
    expand_up(S, own, lambda r: pl.when(r == 2)(lambda: gather(9)))
    contract_grad(S, lambda r: pl.when(r == 2)(lambda: gather(10)))
    R[CON].start()
    G[7].finish()
    hidden_back(S, 0, third)
    G[8].finish()
    hidden_back(S, 1, third)
    R[CON].merge_core()
    gather(11)
    R[CON].two.start()
    G[9].finish()
    hidden_back(S, 2, third)

    S.layer[...] = S.middle[...].astype(BF)
    second_back(S)
    heads_back(S)
    for g in G:
        g.drain()
    for c in range(2):
        every(save[c], "wait")

    def pair_back(p):
        attend_back_pair(S, p)
        pl.when(p == 4)(R[CON].after_two)

    loop(pairs, pair_back)
    first_back(S)
    tokens.start()
    small.start(0)
    load_other(0).start()
    for c in range(2):
        every(reload[c], "start")
    expand_grad(S)
    R[EXP].start()
    R[CON].after_one()
    outproj_grad(S)
    inproj_grad(S)
    R[ATT].start()
    R[EXP].after_core()
    contract_down(S, own)
    put_own.start()

    def rounds():
        for i in range(2, 3 + len(L.more)):
            small.after(i)

    steps = {
        (0, 0): [R[ATT].after_core],
        (0, 3): [lambda: small.after(0)],
        (0, 6): [lambda: small.after(1)],
        (0, 7): [lambda: tokens.forward(1)],
        (0, 9): [R[CON].after_z],
        (1, 0): [R[EXP].after_two, R[CON].after_back_one],
        (1, 1): [R[ATT].after_two],
        (1, 3): [R[CON].after_back_two, rounds],
        (1, 4): [R[EXP].after_one],
        (1, 7): [R[ATT].after_one, lambda: tokens.forward(2)],
        (2, 1): [R[EXP].after_z],
        (2, 3): [R[EXP].after_back_one],
        (2, 4): [small.finish],
        (2, 5): [R[ATT].after_z, R[EXP].after_back_two],
        (2, 7): [R[ATT].after_back_one],
        (2, 8): [R[ATT].after_back_two],
    }

    def at(i, q):
        for (si, sq), fs in steps.items():
            if isinstance(q, int):
                if sq == q:
                    pl.when(i == si)(lambda fs=fs: [f() for f in fs] and None)
            elif 1 <= sq <= pairs:
                pl.when((i == si) & (q == sq))(lambda fs=fs: [f() for f in fs] and None)

    def forward_other(i):
        load_other(i).wait()
        pl.when(i == 0)(lambda: every(reload[ATT], "wait"))
        segment_tables(S, L.peer(i + 1))
        first_norm(S, other)
        for c in range(3):
            project(S, other, c)
        at(i, 0)

        def pair_other(p):
            attend_pair(S, other, p)
            at(i, p + 1)

        loop(pairs, pair_other)
        attend_out(S, other)
        pl.when(i < NZ - 2)(lambda: load_other(i + 1).start())
        at(i, 7)
        pl.when(i == 0)(lambda: every(reload[EXP], "wait"))
        expand_up(S, other)
        at(i, 8)
        pl.when(i > 0)(lambda: put_other(i - 1).wait())
        pl.when(i == 0)(put_own.wait)
        contract_down(S, other)
        put_other(i).start()
        at(i, 9)

    loop(NZ - 1, forward_other)
    put_other(NZ - 2).wait()
    for r in R:
        r.finish()
    tokens.finish()


def run_layer(n_dp, tokens, cot, segments, wi, wo, we, wc, *vectors):
    _, t, d = tokens.shape
    more = max(n_dp.bit_length() - 1 - 3, 0)
    spare = max(more, 1)
    any_, vmem = pl.BlockSpec(memory_space=pl.ANY), pl.BlockSpec(memory_space=pltpu.VMEM)
    V, DMA = pltpu.VMEM, pltpu.SemaphoreType.DMA
    scratch = dict(
        x=V((t, d), BF),
        up=V((t, d), BF),
        normed=V((t, d), BF),
        proj=V((t, 3 * d), BF),
        heads=V((t, d), BF),
        pool=V(((d // 64 + 2 * NZ) * t, d), BF),
        middle=V((t, d), F32),
        second=V((t, d), BF),
        branch=V((t, d), BF),
        gheads=V((t, d), BF),
        seg_col=V((t, 128), F32),
        sums=V((NZ, 16, d), F32),
        layer=V((t, d), BF),
        inv_sum=V((t, 128), F32),
        wbuf=V((3, NZ, d, d), BF),
        con_grad=V((NZ, d, d), BF),
        table=V((16, d), F32),
        bias=V((NZ, 8, d), F32),
        qkv_bias=V((8, d), F32),
        small=V((16, d), F32),
        small_in=V((3 + more, 16, d), F32),
        small_out=V((3 + more, 16, d), F32),
        r1=V((3, NZ, d, d // 2), BF),
        r2=V((NZ, d // 2, d // 2), BF),
        r3=V((NZ, d // 4, d // 2), BF),
        r4=V((3, NZ - 1, d // 4, d // 2), BF),
        r5=V((3, spare, d // 4 if more else 16, d // 2), BF),
        lsem=DMA((13,)),
        gsend=DMA((10, 8)),
        grecv=DMA((10, 8)),
        rsend=DMA((3, 11 + spare)),
        rrecv=DMA((3, 11 + spare)),
        osend=DMA((6,)),
        orecv=DMA((6,)),
        saved=DMA((2, NZ)),
        loaded=DMA((2, NZ)),
        ssend=DMA((6 + more,)),
        srecv=DMA((6 + more,)),
        bsend=DMA((3,)),
        brecv=DMA((3,)),
    )
    names = NAMES_IN + NAMES_OUT + tuple(scratch)
    out_shape = [
        jax.ShapeDtypeStruct((NZ, t, d), BF),
        jax.ShapeDtypeStruct((NZ, t, d), BF),
        jax.ShapeDtypeStruct((d, d), BF),
        jax.ShapeDtypeStruct((d, d), BF),
        jax.ShapeDtypeStruct((d, d), BF),
        jax.ShapeDtypeStruct((16, d), F32),
        jax.ShapeDtypeStruct((2, NZ, d, d), BF),
    ]
    return pl.pallas_call(
        functools.partial(layer_kernel, n_dp, names),
        out_shape=out_shape,
        in_specs=[any_, any_, vmem, any_, any_, any_, any_] + [vmem] * len(vectors),
        out_specs=[any_] * 5 + [vmem, any_],
        scratch_shapes=list(scratch.values()),
        compiler_params=pltpu.CompilerParams(
            collective_id=0, has_side_effects=True, vmem_limit_bytes=63 << 20
        ),
        name="layer",
    )(tokens, cot, segments, wi, wo, we, wc, *vectors)


def local(
    n_dp,
    tokens,
    segments,
    cotangent,
    inproj,
    querybias,
    valuebias,
    outproj,
    outbias,
    gainone,
    shiftone,
    gaintwo,
    shifttwo,
    expand,
    expandbias,
    contract,
    contractbias,
):
    _, t, d = tokens.shape
    w = d // NZ
    wi = inproj.transpose(1, 2, 0).reshape(3 * w, d)
    vectors = (querybias, valuebias, expandbias, outbias, gainone, shiftone, gaintwo, shifttwo, contractbias)
    layers, token_grads, g_att, g_exp, g_con, vec, _ = run_layer(n_dp, tokens, cotangent, segments, wi, outproj, expand, contract, *vectors)
    return (
        layers,
        token_grads,
        g_att[: 3 * w].astype(F32).reshape(3, w, d).transpose(2, 0, 1),
        vec[1, :w],
        vec[2, :w],
        g_att[3 * w :].astype(F32),
        vec[5],
        vec[6],
        vec[7],
        vec[8],
        vec[9],
        g_exp.astype(F32),
        vec[0],
        g_con.astype(F32),
        vec[4],
    )


def solution(mesh):
    in_specs = (
        P("dp", None, None),
        P("dp", None),
        P("dp", None, None),
        P(None, None, "tensor"),
        P("tensor"),
        P("tensor"),
        P("tensor", None),
        P(),
        P(),
        P(),
        P(),
        P(),
        P(None, "tensor"),
        P("tensor"),
        P("tensor", None),
        P(),
    )
    out_specs = (
        P("dp", None, None),
        P("dp", None, None),
        P(None, None, "tensor"),
        P("tensor"),
        P("tensor"),
        P("tensor", None),
        P(),
        P(),
        P(),
        P(),
        P(),
        P(None, "tensor"),
        P("tensor"),
        P("tensor", None),
        P(),
    )
    return jax.shard_map(
        functools.partial(local, mesh.shape["dp"]),
        mesh=mesh,
        in_specs=in_specs,
        out_specs=out_specs,
        check_vma=False,
    )
```

```python
import functools

import jax
import jax.numpy as jnp
from jax import lax
from jax.experimental import pallas as pl
from jax.experimental.pallas import tpu as pltpu
from jax.sharding import PartitionSpec as P

BF = jnp.bfloat16
F32 = jnp.float32
EPSILON = 1e-06
LOG2E = 1.4426950408889634
ROOT_HALF = 0.7071067811865476
INV_ROOT_TWO_PI = 0.3989422804014327
MESH = pl.DeviceIdType.MESH
RT = 192
APART = 2.0**100
NZ = 4
OUT_BIAS, GAIN_ONE, SHIFT_ONE, GAIN_TWO, SHIFT_TWO, CONTRACT_BIAS = range(6)
ATT, EXP, CON = range(3)


def nt(a, b):
    return lax.dot_general(a, b, (((1,), (1,)), ((), ())), preferred_element_type=F32)


def nn(a, b):
    return lax.dot_general(a, b, (((1,), (0,)), ((), ())), preferred_element_type=F32)


def tn(a, b):
    return lax.dot_general(a, b, (((0,), (0,)), ((), ())), preferred_element_type=F32)


def at128(i):
    return pl.ds(pl.multiple_of(i * 128, 128), 128)


def at256(i):
    return pl.ds(pl.multiple_of(i * 256, 256), 256)


def rows(i):
    return pl.ds(pl.multiple_of(i * RT, RT), RT)


def loop(n, f):
    def body(i, carry):
        f(i)
        return carry

    lax.fori_loop(0, n, body, 0)


def standardize(v):
    mu = jnp.mean(v, -1, keepdims=True)
    c = v - mu
    inv = lax.rsqrt(jnp.mean(c * c, -1, keepdims=True) + EPSILON)
    return c * inv, inv


def norm_back(z, unit, inv, gain):
    s = z * gain
    a = jnp.mean(s, -1, keepdims=True)
    b = jnp.mean(s * unit, -1, keepdims=True)
    return inv * (s - a - unit * b)


def head_lanes(shape, h):
    lane = lax.broadcasted_iota(jnp.int32, shape, 1)
    return (lane < 64) if h == 0 else (lane >= 64)


class Bag:
    pass


def segment_column(S, t):
    row = S.segments[pl.ds(t, 1), :].astype(F32)
    S.seg_col[...] = jnp.broadcast_to(row, (128, S.t)).T


def segment_tables(S, t):
    segment_column(S, t)
    lane = lax.broadcasted_iota(jnp.int32, (S.t, 128), 1)
    ids = S.seg_col[...].astype(jnp.int32)
    for h in (0, 1):
        at = lane - (64 if h == 0 else 0)
        same = at == ids
        S.seg_q[h][...] = jnp.where(same, 1.0, 0.0).astype(BF)
        S.seg_k[h][...] = jnp.where((at >= 0) & (at < 8) & (~same), -APART, 0.0).astype(BF)


def first_norm(S, B):
    u, _ = standardize(B.x[...].astype(F32))
    B.normed[...] = (
        u * S.vec[GAIN_ONE : GAIN_ONE + 1, :] + S.vec[SHIFT_ONE : SHIFT_ONE + 1, :]
    ).astype(BF)


def set_bias(S):
    placed = S.bias[0]
    for r in range(1, NZ):
        placed = placed + pltpu.roll(S.bias[r], r * (S.d // NZ), 1)
    S.qkv_bias[...] = placed


def part_matrix(S, B, c):
    w = S.d // NZ
    return jnp.concatenate([B.weight(ATT, r)[c * w : (c + 1) * w, :] for r in range(NZ)], 0)


def project(S, B, c):
    y = nt(B.normed[...], part_matrix(S, B, c)) + S.qkv_bias[c : c + 1, :]
    B.proj[:, c * S.d : (c + 1) * S.d] = y.astype(BF)


def attend_pair(S, B, p):
    n = S.d // 128
    k2 = B.proj[:, at128(n + p)]
    v2 = B.proj[:, at128(2 * n + p)]
    q2 = B.proj[:, at128(p)]
    lane = lax.broadcasted_iota(jnp.int32, (S.t, 128), 1)
    outs, sums = [], []
    for h in (0, 1):
        own = head_lanes(q2.shape, h)
        one = lane == (64 if h == 0 else 0)
        flat = S.keys_t[h]
        flat[...] = jnp.where(own, k2, S.seg_k[h][...]).T
        s = nn(jnp.where(own, q2, S.seg_q[h][...]), flat[...])
        e = jnp.exp2((s - jnp.max(s, -1, keepdims=True)) * (0.125 * LOG2E)).astype(BF)
        if B.keep:
            S.probs(2 * p + h)[...] = e
        o = nn(e, jnp.where(own, v2, jnp.where(one, 1.0, 0.0).astype(BF)))
        at = 64 if h == 0 else 0
        sums.append(1.0 / o[:, at : at + 1])
        outs.append(o)
    first = head_lanes(outs[0].shape, 0)
    scale = jnp.where(first, sums[0], sums[1])
    if B.keep:
        kept = jnp.where(lane == 2 * p, sums[0], S.inv_sum[...])
        S.inv_sum[...] = jnp.where(lane == 2 * p + 1, sums[1], kept)
    B.heads[:, at128(p)] = (jnp.where(first, outs[0], outs[1]) * scale).astype(BF)


def attend_out(S, B):
    m = B.x[...].astype(F32) + nn(B.heads[...], part_matrix(S, B, 3)) + S.vec[OUT_BIAS : OUT_BIAS + 1, :]
    B.middle[...] = m
    u, _ = standardize(m)
    B.second[...] = (
        u * S.vec[GAIN_TWO : GAIN_TWO + 1, :] + S.vec[SHIFT_TWO : SHIFT_TWO + 1, :]
    ).astype(BF)


def expand_up(S, B, done=lambda r: None):
    def g(r):
        w = B.weight(EXP, r)
        for j in range(S.d // 256):
            c = slice(256 * j, 256 * j + 256)
            h = nn(B.second[...], w[:, c]) + S.bias[r, 3:4, c]
            cdf = 0.5 + 0.5 * lax.erf(h * ROOT_HALF)
            B.active(r)[:, c] = (h * cdf).astype(BF)
            if B.keep:
                S.slope(r)[:, c] = (cdf + h * jnp.exp2(h * h * (-0.5 * LOG2E)) * INV_ROOT_TWO_PI).astype(BF)
        done(r)

    loop(NZ, g)


def contract_down(S, B):
    a = (S.layer if B.keep else B.middle)[...].astype(F32) + S.vec[CONTRACT_BIAS : CONTRACT_BIAS + 1, :]
    for r in range(NZ):
        a = a + nn(B.active(r)[...], B.weight(CON, r)[...])
    S.layer[...] = a.astype(BF)


def mask_upstream(S):
    S.small[...] = jnp.zeros_like(S.small)
    g = jnp.where(S.seg_col[:, 0:1] > 0.0, S.up[...].astype(F32), 0.0)
    S.up[...] = g.astype(BF)
    S.small[4:5, :] = jnp.sum(g, 0, keepdims=True)


def hidden_back(S, j, n):
    c = slice(n * j, n * j + n)

    def f(r):
        gh = (nt(S.up[...], S.wbuf[CON, r, c, :]) * S.slope(r)[:, c].astype(F32)).astype(BF)
        S.slope(r)[:, c] = gh
        S.small[pl.ds(r, 1), c] = jnp.sum(gh.astype(F32), 0, keepdims=True)

    loop(NZ, f)


def contract_grad(S, done):
    def f(r):
        S.con_grad[r] = tn(S.own.active(r)[...], S.up[...]).astype(BF)
        done(r)

    loop(NZ, f)


def second_back(S):
    n = S.t // 2
    for k in (8, 9, 5):
        S.small[k : k + 1, :] = jnp.zeros((1, S.d), F32)

    def f(i):
        at = pl.ds(pl.multiple_of(i * n, 32), n)
        gs = nt(S.slope(0)[at, :], S.w[EXP][0])
        for r in range(1, NZ):
            gs = gs + nt(S.slope(r)[at, :], S.w[EXP][r])
        u, inv = standardize(S.middle[at, :])
        gm = S.up[at, :].astype(F32) + norm_back(gs, u, inv, S.vec[GAIN_TWO : GAIN_TWO + 1, :])
        S.middle[at, :] = gm
        gb = gm.astype(BF)
        S.branch[at, :] = gb
        S.small[8:9, :] += jnp.sum(gs * u, 0, keepdims=True)
        S.small[9:10, :] += jnp.sum(gs, 0, keepdims=True)
        S.small[5:6, :] += jnp.sum(gb.astype(F32), 0, keepdims=True)

    loop(2, f)


def expand_grad(S):
    def f(r):
        S.w[EXP][r] = tn(S.second[...], S.slope(r)[...]).astype(BF)

    loop(NZ, f)


def heads_back(S):
    S.gheads[...] = nt(S.branch[...], part_matrix(S, S.own, 3)).astype(BF)


def store_part(S, c, v):
    w = S.d // NZ
    for r in range(NZ):
        S.w[ATT][r, c * w : (c + 1) * w, :] = v[r * w : (r + 1) * w, :]


def outproj_grad(S):
    store_part(S, 3, tn(S.heads[...], S.branch[...]).astype(BF))


def attend_back_pair(S, p):
    n = S.d // 128
    q2 = S.proj[:, at128(p)]
    k2 = S.proj[:, at128(n + p)]
    v2 = S.proj[:, at128(2 * n + p)]
    lane = lax.broadcasted_iota(jnp.int32, (S.t, 128), 1)
    values = S.values_t
    values[...] = v2.T
    kept = S.inv_sum[...]
    scale = [jnp.sum(jnp.where(lane == 2 * p + h, kept, 0.0), -1, keepdims=True) for h in (0, 1)]
    first = head_lanes(q2.shape, 0)
    g2 = (S.gheads[:, at128(p)].astype(F32) * jnp.where(first, scale[0], scale[1])).astype(BF)
    od = g2.astype(F32) * S.heads[:, at128(p)].astype(F32)
    none = jnp.zeros_like(q2)
    dq = None
    for h in (0, 1):
        own = head_lanes(q2.shape, h)
        gm = jnp.where(own, g2, none)
        S.pair_g[h][...] = gm
        S.pair_q[h][...] = jnp.where(own, q2, none)
        dot_sum = jnp.sum(jnp.where(own, od, 0.0), -1, keepdims=True)
        ds = (S.probs(2 * p + h)[...].astype(F32) * (nn(gm, values[...]) - dot_sum)).astype(BF)
        S.pair_s[h][...] = ds
        y = nn(ds, jnp.where(own, k2, none))
        dq = y if dq is None else dq + y
    S.proj[:, at128(p)] = (dq * 0.125).astype(BF)
    dk = tn(S.pair_q[0][...], S.pair_s[0][...]) + tn(S.pair_q[1][...], S.pair_s[1][...])
    dv = tn(S.pair_g[0][...], S.probs(2 * p)[...]) + tn(S.pair_g[1][...], S.probs(2 * p + 1)[...])
    S.proj[:, at128(n + p)] = (dk.T * 0.125).astype(BF)
    S.proj[:, at128(2 * n + p)] = dv.T.astype(BF)


def first_back(S):
    n = S.t // 2
    for k in (6, 7, 10, 11):
        S.small[k : k + 1, :] = jnp.zeros((1, S.d), F32)

    def f(i):
        at = pl.ds(pl.multiple_of(i * n, 32), n)
        gf = None
        for c in range(3):
            y = nn(S.proj[at, c * S.d : (c + 1) * S.d], part_matrix(S, S.own, c))
            gf = y if gf is None else gf + y
        u, inv = standardize(S.x[at, :].astype(F32))
        S.grad[at, :] = (S.middle[at, :] + norm_back(gf, u, inv, S.vec[GAIN_ONE : GAIN_ONE + 1, :])).astype(BF)
        S.small[6:7, :] += jnp.sum(gf * u, 0, keepdims=True)
        S.small[7:8, :] += jnp.sum(gf, 0, keepdims=True)
        S.small[10:11, :] += jnp.sum(S.proj[at, 0 : S.d].astype(F32), 0, keepdims=True)
        S.small[11:12, :] += jnp.sum(S.proj[at, 2 * S.d : 3 * S.d].astype(F32), 0, keepdims=True)

    loop(2, f)


def inproj_grad(S):
    for c in range(3):
        store_part(S, c, tn(S.proj[:, c * S.d : (c + 1) * S.d], S.normed[...]).astype(BF))


class Links:
    def __init__(self, n_dp):
        self.dp = lax.axis_index("dp")
        self.t = lax.axis_index("tensor")
        self.c = self.dp % 2
        bx = (self.dp // 2) % 2
        by = (self.dp // 4) % 2
        self.b1 = bx + self.c * (by - bx)
        self.b2 = by + self.c * (bx - by)
        self.sib = self.dp + 1 - 2 * self.c
        self.p1 = self.dp + (1 - 2 * self.b1) * (2 + 2 * self.c)
        self.p2 = self.dp + (1 - 2 * self.b2) * (4 - 2 * self.c)
        self.more = []
        step = 8
        while step < n_dp:
            self.more.append(self.dp + (1 - 2 * ((self.dp // step) % 2)) * step)
            step *= 2

    def peer(self, r):
        return (self.t + r) % NZ

    def to(self, dp=None, t=None):
        return {"dp": self.dp if dp is None else dp, "tensor": self.t if t is None else t}


def remote(src, dst, ssem, rsem, to):
    return pltpu.make_async_remote_copy(
        src_ref=src, dst_ref=dst, send_sem=ssem, recv_sem=rsem, device_id=to, device_id_type=MESH
    )


class Gather:
    def __init__(self, S, L, k, chunk, base, n):
        d = S.d
        ch = k
        q, h = n // 4, d // 2
        cols = pl.ds(pl.multiple_of(L.c * h, 128), h)
        w = S.w[chunk]

        def quarter(k):
            return pl.ds(base + pl.multiple_of(k * q, 16), q)

        mine = quarter(2 * L.b2 + L.b1)
        near = quarter(2 * L.b2 + 1 - L.b1)
        upper = pl.ds(base + pl.multiple_of(L.b2 * 2 * q, 16), 2 * q)
        lower = pl.ds(base + pl.multiple_of((1 - L.b2) * 2 * q, 16), 2 * q)
        ss, rs = S.gsend, S.grecv
        src = w.at[0]
        self.z = [
            remote(src.at[mine, cols], w.at[r, mine, cols], ss.at[ch, r - 1], rs.at[ch, r - 1], L.to(t=L.peer(NZ - r)))
            for r in range(1, NZ)
        ]
        far = pl.ds(1, NZ - 1)
        self.one = remote(w.at[far, mine, cols], w.at[far, mine, cols], ss.at[ch, 3], rs.at[ch, 3], L.to(dp=L.p1))
        self.two = remote(w.at[far, upper, cols], w.at[far, upper, cols], ss.at[ch, 4], rs.at[ch, 4], L.to(dp=L.p2))
        self.sib = [
            remote(w.at[far, k, cols], w.at[far, k, cols], ss.at[ch, 5 + i], rs.at[ch, 5 + i], L.to(dp=L.sib))
            for i, k in enumerate((mine, near, lower))
        ]

    def start(self):
        for k in self.z:
            k.start()

    def after_z(self):
        for k in self.z:
            k.wait_recv()
        self.one.start()
        self.sib[0].start()

    def after_one(self):
        self.one.wait_recv()
        self.two.start()
        self.sib[1].start()

    def after_two(self):
        self.two.wait_recv()
        self.sib[2].start()

    def finish(self):
        for k in self.sib:
            k.wait_recv()

    def drain(self):
        for k in self.z + [self.one, self.two] + self.sib:
            k.wait_send()


class Reduce:
    def __init__(self, S, L, ch):
        d = S.d
        q, h = d // 4, d // 2
        self.S, self.L, self.ch, self.q, self.h = S, L, ch, q, h
        w = S.con_grad if ch == CON else S.w[ch]
        self.w = w
        self.c0 = pl.multiple_of(L.c * h, 128)
        cols = pl.ds(self.c0, h)
        other = pl.ds(pl.multiple_of((1 - L.c) * h, 128), h)
        self.cols = cols

        def quarter(k):
            return pl.ds(pl.multiple_of(k * q, 64), q)

        self.q0 = pl.multiple_of((2 * L.b2 + L.b1) * q, 64)
        mine = pl.ds(self.q0, q)
        near = quarter(2 * L.b2 + 1 - L.b1)
        self.u0 = pl.multiple_of(L.b2 * h, 128)
        upper = pl.ds(self.u0, h)
        lower = pl.ds(pl.multiple_of((1 - L.b2) * h, 128), h)
        ss, rs = S.rsend, S.rrecv
        out = (S.g_att, S.g_exp, S.g_con)[ch]
        self.core = remote(w.at[:, :, other], S.r1.at[ch], ss.at[ch, 0], rs.at[ch, 0], L.to(dp=L.sib))
        late = {EXP: 0, ATT: 1}.get(ch)
        self.r2 = S.r2 if late is None else S.r1.at[CON, :, late * h : late * h + h]
        self.r3 = S.r3 if late is None else S.r2.at[:, late * q : late * q + q]
        self.two = remote(w.at[:, lower, cols], self.r2, ss.at[ch, 1], rs.at[ch, 1], L.to(dp=L.p2))
        self.one = remote(w.at[:, near, cols], self.r3, ss.at[ch, 2], rs.at[ch, 2], L.to(dp=L.p1))
        self.z = [
            remote(w.at[r, mine, cols], S.r4.at[ch, NZ - 1 - r], ss.at[ch, 2 + r], rs.at[ch, 6 - r], L.to(t=L.peer(r)))
            for r in range(1, NZ)
        ]
        self.more = [
            remote(S.r4.at[ch, i], S.r5.at[ch, i], ss.at[ch, 11 + i], rs.at[ch, 11 + i], L.to(dp=m))
            for i, m in enumerate(L.more)
        ]
        own = w.at[0, mine, cols]
        self.keep = pltpu.make_async_copy(own, out.at[mine, cols], S.lsem.at[3 + ch])
        self.back_one = remote(own, out.at[mine, cols], ss.at[ch, 6], rs.at[ch, 6], L.to(dp=L.p1))
        self.back_two = remote(out.at[upper, cols], out.at[upper, cols], ss.at[ch, 7], rs.at[ch, 7], L.to(dp=L.p2))
        self.back_sib = [
            remote(own, out.at[mine, cols], ss.at[ch, 8], rs.at[ch, 8], L.to(dp=L.sib)),
            remote(out.at[near, cols], out.at[near, cols], ss.at[ch, 9], rs.at[ch, 9], L.to(dp=L.sib)),
            remote(out.at[lower, cols], out.at[lower, cols], ss.at[ch, 10], rs.at[ch, 10], L.to(dp=L.sib)),
        ]

    def start(self):
        self.core.start()

    def add(self, src, first, count):
        w, cols = self.w, self.cols
        step = self.q

        def f(i):
            r, k = i // (count // step), i % (count // step)
            at = pl.ds(first + pl.multiple_of(k * step, 64), step)
            got = src[r, pl.ds(pl.multiple_of(k * step, 64), step), :].astype(F32)
            w[r, at, cols] = (w[r, at, cols].astype(F32) + got).astype(BF)

        loop(NZ * (count // step), f)

    def merge_core(self):
        self.core.wait()
        self.add(self.S.r1.at[self.ch], 0, 2 * self.h)

    def after_core(self):
        self.merge_core()
        self.two.start()

    def after_two(self):
        self.two.wait()
        self.add(self.r2, self.u0, self.h)
        self.one.start()

    def after_one(self):
        self.one.wait()
        self.add(self.r3, self.q0, self.q)
        for k in self.z:
            k.start()

    def after_z(self):
        S, w = self.S, self.w
        for k in self.z:
            k.wait()
        mine = pl.ds(self.q0, self.q)
        v = w[0, mine, self.cols].astype(F32)
        for k in range(NZ - 1):
            v = v + S.r4[self.ch, k].astype(F32)
        for i, k in enumerate(self.more):
            S.r4[self.ch, i] = v.astype(BF)
            k.start()
            k.wait()
            v = S.r4[self.ch, i].astype(F32) + S.r5[self.ch, i].astype(F32)
        w[0, mine, self.cols] = v.astype(BF)
        self.keep.start()
        self.back_one.start()
        self.back_sib[0].start()

    def after_back_one(self):
        self.keep.wait()
        self.back_one.wait()
        self.back_two.start()
        self.back_sib[1].start()

    def after_back_two(self):
        self.back_two.wait()
        self.back_sib[2].start()

    def finish(self):
        for k in self.back_sib:
            k.wait()


class Spread:
    def __init__(self, S, L, own, out):
        self.t = L.t
        right, left = L.to(t=(L.t + 1) % NZ), L.to(t=(L.t + NZ - 1) % NZ)
        ss, rs = S.osend, S.orecv

        def block(j):
            return out.at[(L.t + j + NZ) % NZ]

        self.keep = pltpu.make_async_copy(own, out.at[L.t], S.lsem.at[6])
        self.side = [
            [remote(own if i == 0 else block(-i), block(-i), ss.at[i], rs.at[i], right) for i in range(NZ - 1)],
            [remote(own if i == 0 else block(i), block(i), ss.at[3 + i], rs.at[3 + i], left) for i in range(NZ - 1)],
        ]

    def when_sent(self, i, f):
        pl.when((self.t >= i) & (self.t < NZ - 1))(lambda: f(self.side[0][i]))
        pl.when((self.t <= NZ - 1 - i) & (self.t > 0))(lambda: f(self.side[1][i]))

    def start(self):
        self.keep.start()
        self.send(0)

    def send(self, i):
        self.when_sent(i, lambda k: k.start())

    def arrive(self, i):
        pl.when(self.t >= i + 1)(lambda: self.side[0][i].wait_recv())
        pl.when(self.t <= NZ - 2 - i)(lambda: self.side[1][i].wait_recv())

    def forward(self, i):
        self.arrive(i - 1)
        self.send(i)

    def finish(self):
        self.keep.wait()
        self.arrive(NZ - 2)
        for i in range(NZ - 1):
            self.when_sent(i, lambda k: k.wait_send())


class SmallSum:
    def __init__(self, S, L):
        self.S = S
        ss, rs = S.ssend, S.srecv
        partners = [L.sib, L.p1, L.p2] + L.more
        self.rounds = [
            remote(S.small_out.at[i], S.small_in.at[i], ss.at[i], rs.at[i], L.to(dp=p)) for i, p in enumerate(partners)
        ]
        n = len(partners)
        self.L = L
        self.z = [
            remote(S.small, S.sums.at[L.t], ss.at[n + r - 1], rs.at[n + NZ - 1 - r], L.to(t=L.peer(r)))
            for r in range(1, NZ)
        ]

    def start(self, i):
        self.S.small_out[i] = self.S.small[...]
        self.rounds[i].start()

    def after(self, i):
        self.rounds[i].wait()
        self.S.small[...] += self.S.small_in[i]
        if i + 1 < len(self.rounds):
            self.start(i + 1)
        else:
            for k in self.z:
                k.start()

    def finish(self):
        S, t = self.S, self.L.t
        for k in self.z:
            k.wait()
        S.sums[t] = S.small[...]
        total = S.sums[0] + S.sums[1] + S.sums[2] + S.sums[3]
        S.vec_out[...] = total
        w = S.d // NZ
        hidden = jnp.zeros((1, S.d), F32)
        heads = jnp.zeros((8, S.d), F32)
        for k in range(NZ):
            r = (t + NZ - k) % NZ
            hidden = hidden + S.sums[k, pl.ds(r, 1), :]
            heads = heads + pltpu.roll(S.sums[k, 8:16, :], ((NZ - r) % NZ) * w, 1)
        S.vec_out[0:1, :] = hidden
        S.vec_out[1:3, :] = heads[2:4, :]


NAMES_IN = ("tokens", "cot", "segments", "wi", "wo", "we", "wc", "qb", "vb", "eb", "ob", "g1", "s1", "g2", "s2", "cb")
NAMES_OUT = ("layers", "token_grads", "g_att", "g_exp", "g_con", "vec_out", "kept")


def layer_kernel(n_dp, names, *refs):
    S = Bag()
    for n, r in zip(names, refs):
        setattr(S, n, r)
    S.t, S.d = S.x.shape
    t, d = S.t, S.d
    n_heads, pairs = d // 64, d // 128
    S.w = [S.wbuf.at[0], S.wbuf.at[1], S.wbuf.at[2]]
    S.vec = S.table.at[pl.ds(8, 8)]
    L = Links(n_dp)

    def pool(first, n):
        return S.pool.at[pl.ds(pl.multiple_of(first, 64), n)]

    S.probs = lambda i: S.pool.at[pl.ds(pl.multiple_of(i * t, 64), t), 0:t]
    S.slope = lambda r: pool((n_heads + NZ + r) * t, t)
    spare = [S.pool.at[(n_heads + NZ + r) * t : (n_heads + NZ + r + 1) * t] for r in range(NZ)]
    S.seg_q = [spare[2].at[:, 128 * h : 128 * h + 128] for h in (0, 1)]
    S.seg_k = [spare[2].at[:, 256 + 128 * h : 384 + 128 * h] for h in (0, 1)]
    S.keys_t = [spare[3].at[128 * h : 128 * h + 128, 0:t] for h in (0, 1)]
    S.pair_s = [S.wbuf.at[EXP, h, 0:t, 0:t] for h in (0, 1)]
    S.pair_g = [S.wbuf.at[EXP, 2, 0:t, 128 * h : 128 * h + 128] for h in (0, 1)]
    S.pair_q = [S.wbuf.at[EXP, 2, 0:t, 256 + 128 * h : 384 + 128 * h] for h in (0, 1)]
    S.values_t = S.wbuf.at[EXP, 3, 0:128, 0:t]
    S.grad = S.up

    own, other = Bag(), Bag()
    own.x, own.normed, own.proj, own.heads, own.middle = S.x, S.normed, S.proj, S.heads, S.middle
    own.second, own.keep, own.active = S.second, True, lambda r: pool((n_heads + r) * t, t)
    own.weight = lambda ch, r: S.wbuf.at[ch, r]
    other.x, other.normed, other.proj, other.heads, other.middle = S.x, S.heads, S.proj, S.gheads, S.middle
    other.second, other.keep, other.active = S.branch, False, S.slope
    other.weight = lambda ch, r: S.wbuf.at[ch, r] if ch == CON else pool((ch * NZ + r) * d, d)
    S.own = own

    barrier = pltpu.get_barrier_semaphore()
    partners = [L.to(dp=p) for p in [L.sib, L.p1, L.p2] + L.more] + [L.to(t=L.peer(r)) for r in range(1, NZ)]
    for p in partners:
        pl.semaphore_signal(barrier, inc=1, device_id=p, device_id_type=MESH)
    w = d // NZ
    shards = [
        pltpu.make_async_copy(S.wi, S.w[ATT].at[0, 0 : 3 * w], S.lsem.at[0]),
        pltpu.make_async_copy(S.wo, S.w[ATT].at[0, 3 * w : 4 * w], S.lsem.at[1]),
        pltpu.make_async_copy(S.we, S.w[EXP].at[0], S.lsem.at[2]),
        pltpu.make_async_copy(S.wc, S.w[CON].at[0], S.lsem.at[7]),
    ]
    load_x = pltpu.make_async_copy(S.tokens.at[L.t], S.x, S.lsem.at[8])
    load_up = pltpu.make_async_copy(S.cot.at[L.t], S.up, S.lsem.at[9])
    for k in shards + [load_x, load_up]:
        k.start()
    save = [[pltpu.make_async_copy(S.wbuf.at[c, r], S.kept.at[c, r], S.saved.at[c, r]) for r in range(NZ)] for c in range(2)]
    reload = [
        [pltpu.make_async_copy(S.kept.at[c, r], other.weight(c, r), S.loaded.at[c, r]) for r in range(NZ)] for c in range(2)
    ]

    def every(copies, what):
        for k in copies:
            getattr(k, what)()

    bias = [
        remote(S.table.at[pl.ds(0, 8)], S.bias.at[r], S.bsend.at[r - 1], S.brecv.at[r - 1], L.to(t=L.peer(NZ - r)))
        for r in range(1, NZ)
    ]
    third = d // 3
    parts = [(ATT, w * i, w) for i in range(NZ)] + [(ch, third * i, third) for ch in (EXP, CON) for i in range(3)]
    G = [Gather(S, L, k, *part) for k, part in enumerate(parts)]
    R = [Reduce(S, L, ch) for ch in range(3)]
    tokens = Spread(S, L, S.grad, S.token_grads)
    small = SmallSum(S, L)
    put_own = pltpu.make_async_copy(S.layer, S.layers.at[L.t], S.lsem.at[10])

    def gather(k):
        n = len(G)
        if k < n:
            G[k].after_z()
            if k + 2 < n:
                G[k + 2].start()
        if 0 <= k - 1 < n:
            G[k - 1].after_one()
        if 0 <= k - 2 < n:
            G[k - 2].after_two()

    def load_other(i):
        return pltpu.make_async_copy(S.tokens.at[L.peer(i + 1)], S.x, S.lsem.at[11])

    def put_other(i):
        return pltpu.make_async_copy(S.layer, S.layers.at[L.peer(i + 1)], S.lsem.at[12])

    S.table[...] = jnp.zeros_like(S.table)
    for row, ref in ((0, S.qb), (2, S.vb), (3, S.eb)):
        S.table[row : row + 1, 0 : ref.shape[0]] = ref[...].astype(F32).reshape(1, ref.shape[0])
    for row, ref in enumerate((S.ob, S.g1, S.s1, S.g2, S.s2, S.cb)):
        S.table[8 + row : 9 + row, :] = ref[...].astype(F32).reshape(1, d)
    S.bias[0] = S.table[0:8, :]
    every(shards[:2], "wait")
    pl.semaphore_wait(barrier, len(partners))
    G[0].start()
    G[1].start()
    every(bias, "start")
    every(shards[2:], "wait")
    segment_tables(S, L.t)
    load_x.wait()
    first_norm(S, own)
    gather(0)
    every(bias, "wait")
    set_bias(S)
    gather(1)
    for c in range(3):
        gather(c + 2)
        G[c].finish()
        project(S, own, c)

    def pair(p):
        attend_pair(S, own, p)
        pl.when(p == 1)(lambda: gather(5))
        pl.when(p == 4)(lambda: gather(6))

    loop(pairs, pair)
    G[3].finish()
    every(save[ATT], "start")
    attend_out(S, own)
    load_up.wait()
    mask_upstream(S)
    gather(7)
    gather(8)
    for k in (4, 5, 6):
        G[k].finish()
    every(save[EXP], "start")
    expand_up(S, own, lambda r: pl.when(r == 2)(lambda: gather(9)))
    contract_grad(S, lambda r: pl.when(r == 2)(lambda: gather(10)))
    R[CON].start()
    G[7].finish()
    hidden_back(S, 0, third)
    G[8].finish()
    hidden_back(S, 1, third)
    R[CON].merge_core()
    gather(11)
    R[CON].two.start()
    G[9].finish()
    hidden_back(S, 2, third)

    S.layer[...] = S.middle[...].astype(BF)
    second_back(S)
    heads_back(S)
    for g in G:
        g.drain()
    for c in range(2):
        every(save[c], "wait")

    def pair_back(p):
        attend_back_pair(S, p)
        pl.when(p == 4)(R[CON].after_two)

    loop(pairs, pair_back)
    first_back(S)
    tokens.start()
    small.start(0)
    load_other(0).start()
    for c in range(2):
        every(reload[c], "start")
    expand_grad(S)
    R[EXP].start()
    R[CON].after_one()
    outproj_grad(S)
    inproj_grad(S)
    R[ATT].start()
    R[EXP].after_core()
    contract_down(S, own)
    put_own.start()

    def rounds():
        for i in range(2, 3 + len(L.more)):
            small.after(i)

    steps = {
        (0, 3): [lambda: small.after(0)],
        (0, 6): [lambda: small.after(1)],
        (0, 7): [lambda: tokens.forward(1)],
        (0, 9): [R[CON].after_z],
        (1, 0): [R[EXP].after_two, R[CON].after_back_one],
        (1, 1): [R[ATT].after_two],
        (1, 3): [R[CON].after_back_two, rounds],
        (1, 4): [R[EXP].after_one],
        (1, 6): [R[ATT].after_one],
        (1, 7): [lambda: tokens.forward(2)],
        (2, 1): [R[EXP].after_z],
        (2, 3): [R[EXP].after_back_one],
        (2, 4): [small.finish],
        (2, 5): [R[ATT].after_z, R[EXP].after_back_two],
        (2, 7): [R[ATT].after_back_one],
        (2, 8): [R[ATT].after_back_two],
    }

    def at(i, q):
        for (si, sq), fs in steps.items():
            if isinstance(q, int):
                if sq == q:
                    pl.when(i == si)(lambda fs=fs: [f() for f in fs] and None)
            elif 1 <= sq <= pairs:
                pl.when((i == si) & (q == sq))(lambda fs=fs: [f() for f in fs] and None)

    def forward_other(i):
        load_other(i).wait()
        pl.when(i == 0)(lambda: every(reload[ATT], "wait"))
        segment_tables(S, L.peer(i + 1))
        first_norm(S, other)
        for c in range(3):
            project(S, other, c)
        at(i, 0)

        def pair_other(p):
            attend_pair(S, other, p)
            at(i, p + 1)

        loop(pairs, pair_other)
        attend_out(S, other)
        pl.when(i < NZ - 2)(lambda: load_other(i + 1).start())
        at(i, 7)
        pl.when(i == 0)(lambda: every(reload[EXP], "wait"))
        expand_up(S, other)
        at(i, 8)
        pl.when(i > 0)(lambda: put_other(i - 1).wait())
        pl.when(i == 0)(put_own.wait)
        contract_down(S, other)
        put_other(i).start()
        at(i, 9)

    R[ATT].after_core()
    loop(NZ - 1, forward_other)
    put_other(NZ - 2).wait()
    for r in R:
        r.finish()
    tokens.finish()


def run_layer(n_dp, tokens, cot, segments, wi, wo, we, wc, *vectors):
    _, t, d = tokens.shape
    more = max(n_dp.bit_length() - 1 - 3, 0)
    spare = max(more, 1)
    any_, vmem = pl.BlockSpec(memory_space=pl.ANY), pl.BlockSpec(memory_space=pltpu.VMEM)
    V, DMA = pltpu.VMEM, pltpu.SemaphoreType.DMA
    scratch = dict(
        x=V((t, d), BF),
        up=V((t, d), BF),
        normed=V((t, d), BF),
        proj=V((t, 3 * d), BF),
        heads=V((t, d), BF),
        pool=V(((d // 64 + 2 * NZ) * t, d), BF),
        middle=V((t, d), F32),
        second=V((t, d), BF),
        branch=V((t, d), BF),
        gheads=V((t, d), BF),
        seg_col=V((t, 128), F32),
        sums=V((NZ, 16, d), F32),
        layer=V((t, d), BF),
        inv_sum=V((t, 128), F32),
        wbuf=V((3, NZ, d, d), BF),
        con_grad=V((NZ, d, d), BF),
        table=V((16, d), F32),
        bias=V((NZ, 8, d), F32),
        qkv_bias=V((8, d), F32),
        small=V((16, d), F32),
        small_in=V((3 + more, 16, d), F32),
        small_out=V((3 + more, 16, d), F32),
        r1=V((3, NZ, d, d // 2), BF),
        r2=V((NZ, d // 2, d // 2), BF),
        r3=V((NZ, d // 4, d // 2), BF),
        r4=V((3, NZ - 1, d // 4, d // 2), BF),
        r5=V((3, spare, d // 4 if more else 16, d // 2), BF),
        lsem=DMA((13,)),
        gsend=DMA((10, 8)),
        grecv=DMA((10, 8)),
        rsend=DMA((3, 11 + spare)),
        rrecv=DMA((3, 11 + spare)),
        osend=DMA((6,)),
        orecv=DMA((6,)),
        saved=DMA((2, NZ)),
        loaded=DMA((2, NZ)),
        ssend=DMA((6 + more,)),
        srecv=DMA((6 + more,)),
        bsend=DMA((3,)),
        brecv=DMA((3,)),
    )
    names = NAMES_IN + NAMES_OUT + tuple(scratch)
    out_shape = [
        jax.ShapeDtypeStruct((NZ, t, d), BF),
        jax.ShapeDtypeStruct((NZ, t, d), BF),
        jax.ShapeDtypeStruct((d, d), BF),
        jax.ShapeDtypeStruct((d, d), BF),
        jax.ShapeDtypeStruct((d, d), BF),
        jax.ShapeDtypeStruct((16, d), F32),
        jax.ShapeDtypeStruct((2, NZ, d, d), BF),
    ]
    return pl.pallas_call(
        functools.partial(layer_kernel, n_dp, names),
        out_shape=out_shape,
        in_specs=[any_, any_, vmem, any_, any_, any_, any_] + [vmem] * len(vectors),
        out_specs=[any_] * 5 + [vmem, any_],
        scratch_shapes=list(scratch.values()),
        compiler_params=pltpu.CompilerParams(
            collective_id=0, has_side_effects=True, vmem_limit_bytes=63 << 20
        ),
        name="layer",
    )(tokens, cot, segments, wi, wo, we, wc, *vectors)


def local(
    n_dp,
    tokens,
    segments,
    cotangent,
    inproj,
    querybias,
    valuebias,
    outproj,
    outbias,
    gainone,
    shiftone,
    gaintwo,
    shifttwo,
    expand,
    expandbias,
    contract,
    contractbias,
):
    _, t, d = tokens.shape
    w = d // NZ
    wi = inproj.transpose(1, 2, 0).reshape(3 * w, d)
    vectors = (querybias, valuebias, expandbias, outbias, gainone, shiftone, gaintwo, shifttwo, contractbias)
    layers, token_grads, g_att, g_exp, g_con, vec, _ = run_layer(n_dp, tokens, cotangent, segments, wi, outproj, expand, contract, *vectors)
    return (
        layers,
        token_grads,
        g_att[: 3 * w].astype(F32).reshape(3, w, d).transpose(2, 0, 1),
        vec[1, :w],
        vec[2, :w],
        g_att[3 * w :].astype(F32),
        vec[5],
        vec[6],
        vec[7],
        vec[8],
        vec[9],
        g_exp.astype(F32),
        vec[0],
        g_con.astype(F32),
        vec[4],
    )


def solution(mesh):
    in_specs = (
        P("dp", None, None),
        P("dp", None),
        P("dp", None, None),
        P(None, None, "tensor"),
        P("tensor"),
        P("tensor"),
        P("tensor", None),
        P(),
        P(),
        P(),
        P(),
        P(),
        P(None, "tensor"),
        P("tensor"),
        P("tensor", None),
        P(),
    )
    out_specs = (
        P("dp", None, None),
        P("dp", None, None),
        P(None, None, "tensor"),
        P("tensor"),
        P("tensor"),
        P("tensor", None),
        P(),
        P(),
        P(),
        P(),
        P(),
        P(None, "tensor"),
        P("tensor"),
        P("tensor", None),
        P(),
    )
    return jax.shard_map(
        functools.partial(local, mesh.shape["dp"]),
        mesh=mesh,
        in_specs=in_specs,
        out_specs=out_specs,
        check_vma=False,
    )
```
